32 devices in a mesh: groups: 2 (over y), ctx: 4 (over z), head: 2 (over x), sub: 2 (over core).
Axes of the slice: x: 2, y: 2, z: 4, core: 2. Of those that a mesh axis runs over, the one named last changes fastest.
Arguments:
- tokens: bfloat16 [8192, 768], P(('groups', 'ctx', 'sub')), parts along dimension 0, may hold values from -6 to 6
- norm_gain: float32 [768], replicated, may hold values from 0.1 to 1.9
- w_qkv: bfloat16 [768, 3, 768], P(None, None, 'head'), may hold values from -0.21875 to 0.21875
- q_gain: float32 [768], P('head'), may hold values from 0.1 to 1.9
- k_gain: float32 [768], P('head'), may hold values from 0.1 to 1.9
- w_out: bfloat16 [768, 768], P('head'), may hold values from -0.21875 to 0.21875
- seg_len: int32 [16], replicated, may hold values from 512 to 4096, as said below
- dilation: int32 [16], replicated, may hold values from 1 to 16, as said below
- slide_len: int32 [16], P('groups'), parts along dimension 0, may hold values from 1 to 2048, 4096 in all
- reports: bfloat16 [256, 768], P(None, 'head'), may hold values from -6 to 6
- pairs: int32 [16], P('groups'), parts along dimension 0, may hold values from 0 to 255
- log_scale: float32 [1], replicated, may hold values from 2.3 to 3.4
Outputs:
- mixed: bfloat16 [8192, 768], P(('groups', 'ctx', 'sub'), 'head'), parts along dimension 0
- similarity: float32 [16, 256], P('groups'), parts along dimension 0
- loss: float32 [16], P('groups'), parts along dimension 0
The draws below stay inside these ranges and needn't reach their ends.
There are 2 independent parts, one for each index of `groups`. The reference program is written for one: setup_inputs(seed, part) draws one part's arguments, and reference() takes and returns one part's arrays. A program takes and returns all parts, laid end to end along the dimension named above; an argument that names none is the same for every part. Nothing has to cross between parts.
Inputs may be any that keep to these rules, and one draw needn't show every extreme that they name: `seg_len`: each is 512 times a power of two; one head's is 4096. `dilation`: each is a power of two; one head's is 16. `slide_len`: they sum to 4096.
All inputs are finite; a program needn't handle non-finite values.
Results may differ from the reference program's by a relative error of at most 0.0033.
The reference program's roundings to bfloat16 on the way count: a program that leaves them out, or rounds other values in their place, can miss the bound.
Values may be sent and summed in bfloat16 or wider, within the bound.
No kernel may reach another device: no remote copies, remote signals or barrier semaphores. Data moves between devices by JAX's collectives and lax.ppermute only.
A program may use at most 64 MiB of HBM per device.

```python
import math
import jax
import jax.numpy as jnp
import numpy as np
from jax import lax

D = 768
HEADS = 16
HEAD_DIM = 48
TOK_DEV = 512
SLIDES = 8
REPORTS = 256
SEQ = 4096


def draw_seg_len(key, part):
    levels = (SEQ // TOK_DEV).bit_length() - 1
    first, second = jax.random.split(jax.random.fold_in(key, 11))
    picks = jax.random.randint(first, (HEADS,), 0, levels + 1)
    chosen = jax.random.randint(second, (), 0, HEADS)
    picks = jnp.where(jnp.arange(HEADS) == chosen, levels, picks)
    return (TOK_DEV * jnp.power(2, picks)).astype(jnp.int32)


def draw_dilation(key, part):
    first, second = jax.random.split(jax.random.fold_in(key, 23))
    picks = jax.random.randint(first, (HEADS,), 0, 5)
    chosen = jax.random.randint(second, (), 0, HEADS)
    picks = jnp.where(jnp.arange(HEADS) == chosen, 4, picks)
    return jnp.power(2, picks).astype(jnp.int32)


def plant(result, key, least, high):
    dims = result.shape
    place = [jax.random.randint(jax.random.fold_in(key, axis), (), 0, dims[axis]) for axis in range(len(dims))]
    result = result.at[tuple(place)].set(least)
    longest = dims.index(max(dims))
    place[longest] = (place[longest] + 1) % dims[longest]
    return result.at[tuple(place)].set(high)


def block_scale(key, dims, pieces, low, top_value):
    factor_of = 1.0
    for dim, shards_of in pieces:
        draws = jax.random.uniform(jax.random.fold_in(jax.random.fold_in(key, 6), dim), (shards_of,), jnp.float32, low / len(pieces), top_value / len(pieces))
        factor_of = factor_of * jnp.repeat(jnp.exp(draws), dims[dim] // shards_of).reshape((-1,) + (1,) * (len(dims) - 1 - dim))
    return factor_of


def split_up(number_of, total, limit, skew):
    loads = [(1 << 20) // math.isqrt(standing ** skew) + 1 for standing in range(2, number_of + 1)]
    rest, counts = total - limit - (number_of - 1), [1] * (number_of - 1)
    while rest > 0:
        candidates = [i for i in range(number_of - 1) if counts[i] < limit]
        pool, budget = sum([loads[i] for i in candidates]), rest
        for i in candidates:
            more = min(limit - counts[i], max(1, budget * loads[i] // pool), rest)
            counts[i] = counts[i] + more
            rest = rest - more
    return np.array([limit] + counts)


def uneven(stream_key, amount, total, reach, skew):
    if amount == 2:
        one = jax.random.randint(stream_key, (), max(1, total - reach), min(reach, total - 1) + 1)
        return jnp.stack([one, total - one])
    sizes = jnp.asarray(split_up(amount, total, reach, skew), jnp.int32)
    couples = (amount - 1) // 2
    giver, receiver = sizes[1:1 + 2 * couples:2], sizes[2:2 + 2 * couples:2]
    margin = jnp.minimum(giver - 1, reach - receiver)
    shifted = jax.random.randint(jax.random.fold_in(stream_key, 1), (couples,), 0, 1 << 20) % (margin + 1)
    sizes = sizes.at[1:1 + 2 * couples:2].set(giver - shifted).at[2:2 + 2 * couples:2].set(receiver + shifted)
    return sizes[jax.random.permutation(jax.random.fold_in(stream_key, 2), amount)]


def gaussian(stream_key, extent, scale, limit, cuts=(), kind=jnp.bfloat16):
    array = scale * jax.random.normal(stream_key, extent, jnp.float32)
    if cuts:
        array = array * block_scale(stream_key, extent, cuts, -0.22, 0.18)
    return jnp.clip(array, -limit, limit).astype(kind)


def setup_inputs(seed: int = 0, part: int = 0) -> dict:
    seeds = jax.random.split(jax.random.key(seed), 13)
    own_keys = jax.random.split(jax.random.fold_in(seeds[12], part), 13)
    tokens = gaussian(own_keys[0], (SEQ, D), 1.0, 6.0, ((0, 8),))
    norm_gain = jnp.clip(1.0 + 0.18 * jax.random.normal(seeds[1], (D,), jnp.float32), 0.1, 1.9)
    w_qkv = gaussian(seeds[2], (D, 3, HEADS * HEAD_DIM), D ** -0.5, 0.21875, ((2, 2),))
    q_gain = jnp.clip(1.0 + 0.18 * jax.random.normal(seeds[3], (HEADS * HEAD_DIM,), jnp.float32), 0.1, 1.9)
    k_gain = jnp.clip(1.0 + 0.18 * jax.random.normal(seeds[4], (HEADS * HEAD_DIM,), jnp.float32), 0.1, 1.9)
    w_out = gaussian(seeds[5], (HEADS * HEAD_DIM, D), (HEADS * HEAD_DIM) ** -0.5, 0.21875, ((0, 2),))
    seg_len = draw_seg_len(jax.random.fold_in(seeds[12], 71), part)
    dilation = draw_dilation(jax.random.fold_in(seeds[12], 71), part)
    slide_len = uneven(own_keys[8], SLIDES, SEQ, SEQ // 2, 2).astype(jnp.int32)
    reports = gaussian(seeds[9], (REPORTS, D), 1.0, 6.0, ((1, 2),))
    pairs = plant(jax.random.randint(own_keys[10], (SLIDES,), 0, REPORTS), jax.random.fold_in(own_keys[10], 1), 0, REPORTS - 1).astype(jnp.int32)
    log_scale = jnp.clip(jax.random.uniform(seeds[11], (1,), jnp.float32, 2.3, 3.4), 2.3, 3.4)
    return dict(tokens=tokens, norm_gain=norm_gain, w_qkv=w_qkv, q_gain=q_gain, k_gain=k_gain, w_out=w_out, seg_len=seg_len, dilation=dilation, slide_len=slide_len, reports=reports, pairs=pairs, log_scale=log_scale)


def slide_of(positions, ends):
    return lax.optimization_barrier(jnp.sum((positions[:, None] >= ends[None, :]).astype(jnp.int32), axis=1)).astype(jnp.int32)

def head_norm(values, gain):
    scale = lax.rsqrt(lax.optimization_barrier(jnp.mean(values * values, axis=-1, keepdims=True)) + 1e-06)
    return (values * scale * gain).astype(jnp.bfloat16)

def reference(tokens, norm_gain, w_qkv, q_gain, k_gain, w_out, seg_len, dilation, slide_len, reports, pairs, log_scale):
    x_full = tokens.astype(jnp.float32)
    mean_sq = lax.optimization_barrier(jnp.mean(x_full * x_full, axis=-1, keepdims=True))
    normed = (x_full * lax.rsqrt(mean_sq + 1e-06) * norm_gain).astype(jnp.bfloat16)
    qkv = jnp.dot(normed, w_qkv.reshape(D, 3 * HEADS * HEAD_DIM), preferred_element_type=jnp.float32)
    qkv = qkv.reshape(SEQ, 3, HEADS, HEAD_DIM)
    qn = head_norm(qkv[:, 0], q_gain.reshape(HEADS, HEAD_DIM))
    kn = head_norm(qkv[:, 1], k_gain.reshape(HEADS, HEAD_DIM))
    vb = qkv[:, 2].astype(jnp.bfloat16)
    positions = jnp.arange(SEQ, dtype=jnp.int32)
    ends = jnp.cumsum(slide_len).astype(jnp.int32)
    sids = slide_of(positions, ends)
    block = math.gcd(SEQ, 512)
    inv_root = 1.0 / math.sqrt(HEAD_DIM)

    def one_head(args):
        head_id, q_head, k_head, v_head, width, rate = args
        offset = jnp.remainder(head_id, rate)
        chosen = jnp.remainder(positions, rate) == offset
        segment = positions // width

        def one_block(carry, start):
            q_blk = lax.dynamic_slice_in_dim(q_head, start, block, 0)
            sel_q = lax.dynamic_slice_in_dim(chosen, start, block, 0)
            seg_q = lax.dynamic_slice_in_dim(segment, start, block, 0)
            sid_q = lax.dynamic_slice_in_dim(sids, start, block, 0)
            scores = jnp.dot(q_blk, k_head.T, preferred_element_type=jnp.float32) * inv_root
            allowed = sel_q[:, None] & chosen[None, :] & (seg_q[:, None] == segment[None, :]) & (sid_q[:, None] == sids[None, :])
            expo = jnp.where(allowed, jnp.exp(scores), jnp.float32(0.0))
            total = lax.optimization_barrier(jnp.sum(expo, axis=1))
            numer = jnp.dot(expo.astype(jnp.bfloat16), v_head, preferred_element_type=jnp.float32)
            safe = jnp.where(total > 0, total, jnp.float32(1.0))
            out = jnp.where(total[:, None] > 0, numer / safe[:, None], jnp.float32(0.0))
            return (carry, out.astype(jnp.bfloat16))
        starts = jnp.arange(SEQ // block, dtype=jnp.int32) * block
        _, outs = lax.scan(one_block, jnp.int32(0), starts)
        return outs.reshape(SEQ, HEAD_DIM)
    head_ids = jnp.arange(HEADS, dtype=jnp.int32)
    per_head = lax.map(one_head, (head_ids, jnp.transpose(qn, (1, 0, 2)), jnp.transpose(kn, (1, 0, 2)), jnp.transpose(vb, (1, 0, 2)), seg_len, dilation))
    head_out = jnp.transpose(per_head, (1, 0, 2)).reshape(SEQ, HEADS * HEAD_DIM)
    proj = jnp.dot(head_out, w_out, preferred_element_type=jnp.float32)
    mixed = (x_full + proj).astype(jnp.bfloat16)
    onehot = (sids[None, :] == jnp.arange(SLIDES, dtype=jnp.int32)[:, None]).astype(jnp.bfloat16)
    sums = jnp.dot(onehot, mixed, preferred_element_type=jnp.float32)
    pooled = sums / slide_len.astype(jnp.float32)[:, None]
    rep = reports.astype(jnp.float32)
    dots = jnp.dot(pooled, rep.T, precision=lax.Precision.HIGHEST)
    slide_sq = lax.optimization_barrier(jnp.sum(pooled * pooled, axis=1))
    report_sq = lax.optimization_barrier(jnp.sum(rep * rep, axis=1))
    scale = jnp.exp(log_scale[0])
    similarity = scale * dots / jnp.sqrt((slide_sq[:, None] + 1e-06) * (report_sq[None, :] + 1e-06))
    total = lax.optimization_barrier(jnp.sum(jnp.exp(similarity - scale), axis=1))
    picked = lax.optimization_barrier(jnp.sum(jnp.where(jnp.arange(REPORTS, dtype=jnp.int32)[None, :] == pairs[:, None], similarity, jnp.float32(0.0)), axis=1))
    loss = scale + jnp.log(total) - picked
    return (mixed, similarity, loss)
```

```python
import functools
import math

import jax
import jax.numpy as jnp
from jax import lax
from jax.experimental import pallas as pl
from jax.experimental.pallas import tpu as pltpu
from jax.sharding import PartitionSpec as P


HEAD_DIM = 48
RES = 16
LANES = 128
HALF = 64
FAR = 4096.0
MIB = 1024 * 1024
F32 = jnp.float32
BF16 = jnp.bfloat16
I32 = jnp.int32


def rev(r):
    return int(f"{r:04b}"[::-1], 2)


def rev_traced(c):
    return ((c & 1) << 3) | ((c & 2) << 1) | ((c >> 1) & 2) | ((c >> 3) & 1)


def dot(a, b, dims=((1,), (0,)), precision=None):
    return lax.dot_general(a, b, (dims, ((), ())), precision=precision, preferred_element_type=F32)


def units_of(dil_ref, h):
    rate = dil_ref[h]
    count = jnp.int32(RES)
    for step in range(1, RES.bit_length()):
        count = jnp.where(rate == 1 << step, RES >> step, count)
    return count


def first_unit(dil_ref, h):
    return rev_traced(jnp.bitwise_and(h, dil_ref[h] - 1))


UNITS, FIRST, OFFSET, REACH, FIELDS = 0, 1, 2, 3, 4
HEAD_AT = 4


def slide_tiles(len_ref, rows, my_start, slides, one, inside, outside):
    per = rows // RES
    base = RES * lax.broadcasted_iota(I32, (per, LANES), 0) + my_start
    lane = lax.broadcasted_iota(I32, (1, LANES), 1)
    tiles = []
    for side in range(2):
        low, high, on = slide_lanes(len_ref, S_AT[side], slides)
        high = jnp.where(on, high, -1)
        other = jnp.where(on, outside, jnp.where(lane == ONE_AT, one, 0.0))
        parts = []
        for u in range(RES):
            tok = base + rev(u)
            parts.append(jnp.where((tok >= low) & (tok < high), inside, other))
        tiles.append(jnp.concatenate(parts, axis=0))
    return tiles


def slide_lanes(ends_ref, base, slides):
    lane = lax.broadcasted_iota(I32, (1, LANES), 1) - base
    low = jnp.zeros((1, LANES), I32)
    high = jnp.zeros((1, LANES), I32)
    end = jnp.int32(0)
    for s in range(slides):
        low = jnp.where(lane == s, end, low)
        end = end + ends_ref[s]
        high = jnp.where(lane == s, end, high)
    return low, high, (lane >= 0) & (lane < slides)


def selector(source, first, heads_at, target):
    lane = lax.broadcasted_iota(I32, (1, 2 * LANES), 1)
    wanted = jnp.full((1, 2 * LANES), -1, I32)
    for side in range(2):
        at = side * LANES + target[side]
        inside = (lane >= at) & (lane < at + HEAD_DIM)
        wanted = jnp.where(inside, (heads_at + side) * HEAD_DIM - first + lane - at, wanted)
    row = lax.broadcasted_iota(I32, (source, 2 * LANES), 0)
    return jnp.where(row == wanted, 1.0, 0.0).astype(BF16)


V_AT = (0, HALF)
K_AT = (HALF, 0)
S_AT = (HALF + HEAD_DIM, HEAD_DIM)
ONE_AT = HALF - 1


def head_scale(values, feat):
    sq = values * values
    high = sq.astype(BF16)
    low = (sq - high.astype(F32)).astype(BF16)
    lane = lax.broadcasted_iota(I32, (1, feat), 1)
    first = jnp.zeros((1, feat), I32)
    for h in range(1, feat // HEAD_DIM):
        first = jnp.where(lane >= h * HEAD_DIM, h * HEAD_DIM, first)
    row = lax.broadcasted_iota(I32, (feat, feat), 0)
    same = jnp.where((row >= first) & (row < first + HEAD_DIM), 1.0, 0.0).astype(BF16)
    return lax.rsqrt((dot(high, same) + dot(low, same)) * (1.0 / HEAD_DIM) + 1e-06)


def span(pair, feat):
    first = pair * 2 * HEAD_DIM // LANES * LANES
    last = ((pair + 1) * 2 * HEAD_DIM - 1) // LANES * LANES + LANES
    return first, min(last, feat) - first


def members(slide_ref, tok, slides):
    row = lax.broadcasted_iota(I32, (slides, 1), 0)
    low = jnp.zeros((slides, 1), I32)
    high = jnp.zeros((slides, 1), I32)
    end = jnp.int32(0)
    for s in range(slides):
        low = jnp.where(row == s, end, low)
        end = end + slide_ref[s]
        high = jnp.where(row == s, end, high)
    return jnp.where((tok >= low) & (tok < high), 1.0, 0.0).astype(BF16)


def keys_kernel(
    ladder, heads, parts, classes, slides, seg_ref, dil_ref, len_ref, x_ref, ng_ref, wk_ref, wv_ref, kg_ref,
    pack_ref, normed_ref, meta_ref, xs_ref, kv_ref,
):
    rows, width = x_ref.shape
    feat = heads * HEAD_DIM
    per = rows // RES
    base = lax.axis_index("head") * heads
    my_start = lax.axis_index(("ctx", "sub")) * rows
    segs = [seg_ref[h] for h in range(parts * heads)]
    counts = [units_of(dil_ref, h) for h in range(parts * heads)]
    fits = [jnp.bool_(True) for _ in ladder]
    for c in range(1, classes + 1):
        most = jnp.int32(0)
        for part in range(parts):
            total = jnp.int32(0)
            for h in range(part * heads, (part + 1) * heads):
                total = total + jnp.where(segs[h] >= (rows << c), counts[h], 0)
            most = jnp.maximum(most, total)
        for i, caps in enumerate(ladder):
            fits[i] = fits[i] & (most <= caps[min(c, len(caps)) - 1])
    tier = jnp.int32(len(ladder) - 1)
    for i in reversed(range(len(ladder))):
        tier = jnp.where(fits[i], i, tier)
    meta_ref[0] = tier
    local_seg = [seg_ref[base + h] for h in range(heads)]
    local_units = [units_of(dil_ref, base + h) for h in range(heads)]
    starts = [first_unit(dil_ref, base + h) for h in range(heads)]
    offset = []
    for h in range(heads):
        total = jnp.int32(0)
        for other in range(heads):
            ahead = local_seg[other] > local_seg[h]
            if other < h:
                ahead = ahead | (local_seg[other] == local_seg[h])
            if other != h:
                total = total + jnp.where(ahead, local_units[other], 0)
        offset.append(total)
        at = HEAD_AT + h * FIELDS
        meta_ref[at + UNITS] = local_units[h]
        meta_ref[at + FIRST] = starts[h] * per
        meta_ref[at + OFFSET] = total * per
        meta_ref[at + REACH] = local_seg[h] // rows

    x = x_ref[...].astype(F32)
    mean_sq = jnp.mean(x * x, axis=-1, keepdims=True)
    normal = x * lax.rsqrt(mean_sq + 1e-06) * ng_ref[...].reshape(1, width)
    for c in range(width // LANES):
        lanes = slice(c * LANES, (c + 1) * LANES)
        xs_ref[c] = normal[:, lanes]
        for r in range(RES):
            at = rev(r) * per
            normed_ref[at : at + per, lanes] = xs_ref[c, pl.ds(r, per, stride=RES), :].astype(BF16)
    normed = normed_ref[...]
    keys = dot(normed, wk_ref[0])
    vals = dot(normed, wv_ref[0]).astype(BF16)
    kn = (keys * head_scale(keys, feat) * kg_ref[...].reshape(1, feat)).astype(BF16)
    extra = slide_tiles(len_ref, rows, my_start, slides, 1.0, 0.0, -FAR)
    for pair in range(heads // 2):
        first, size = span(pair, feat)
        both = dot(kn[:, first : first + size], selector(size, first, 2 * pair, K_AT))
        both = both + dot(vals[:, first : first + size], selector(size, first, 2 * pair, V_AT))
        for side in range(2):
            h = 2 * pair + side
            kv_ref[h] = (both[:, side * LANES : (side + 1) * LANES] + extra[side]).astype(BF16)

    for h in range(heads):

        def put(u, carry, h=h, to=offset[h], at=starts[h]):
            piece = kv_ref[h, pl.ds(pl.multiple_of((at + u) * per, per), per), :]
            pack_ref[pl.ds(pl.multiple_of((to + u) * per, per), per), :] = piece
            return carry

        lax.fori_loop(0, local_units[h], put, 0)


def queries_kernel(
    heads, slides, blocks, len_ref, x_ref, normed_ref, w_ref, qg_ref, w_out_ref, rep_ref, q_ref, sums_ref, wide_ref
):
    rows = normed_ref.shape[0]
    feat = heads * HEAD_DIM
    my_start = lax.axis_index(("ctx", "sub")) * rows
    piece = rows // 4
    per = rows // RES
    base = RES * lax.broadcasted_iota(I32, (per, LANES), 0) + my_start

    def step(i, carry):
        here = pl.ds(pl.multiple_of(i * piece, piece), piece)
        q = dot(normed_ref[here, :], w_ref[0])
        qn = (q * head_scale(q, feat) * qg_ref[...].reshape(1, feat)).astype(BF16)
        extra = []
        for side in range(2):
            low, high, on = slide_lanes(len_ref, S_AT[side], slides)
            high = jnp.where(on, high, -1)
            parts = []
            for u in range(piece // per):
                tok = base + rev_traced(i * (piece // per) + u)
                parts.append(jnp.where((tok >= low) & (tok < high), 1.0, 0.0))
            extra.append(jnp.concatenate(parts, axis=0))
        for pair in range(heads // 2):
            first, size = span(pair, feat)
            both = dot(qn[:, first : first + size], selector(size, first, 2 * pair, K_AT))
            for side in range(2):
                lanes = slice(side * LANES, (side + 1) * LANES)
                q_ref[2 * pair + side, here, :] = (both[:, lanes] + extra[side]).astype(BF16)
        return carry

    lax.fori_loop(0, rows // piece, step, 0)
    place = lax.broadcasted_iota(I32, (1, rows), 1) + my_start
    width = x_ref.shape[1]
    sums_ref[:, :width] = dot(members(len_ref, place, slides), x_ref[...])
    rep = rep_ref[...].astype(F32)
    share = jnp.full((slides, rep.shape[1]), 1.0 / blocks, F32)
    sums_ref[:, width:] = dot(share, rep * rep, ((1,), (1,)), lax.Precision.HIGHEST)
    wide_ref[...] = jnp.zeros_like(wide_ref)
    for h in range(heads):
        at = h // 2 * LANES + V_AT[h % 2]
        wide_ref[at : at + HEAD_DIM, :] = w_out_ref[h * HEAD_DIM : (h + 1) * HEAD_DIM, :]


def attend_kernel(heads, blocks, slides, meta_ref, len_ref, q_ref, *rest):
    kv_refs = rest[:blocks]
    out_ref, kvs_ref, keys_ref, acc_ref, list_ref, before_ref, sem = rest[blocks:]
    rows = q_ref.shape[1]
    per = rows // RES
    me = lax.axis_index(("ctx", "sub"))
    copies = []
    for m in range(blocks):
        size = kv_refs[m].shape[0]
        copies.append(pltpu.make_async_copy(kv_refs[m], kvs_ref.at[m, pl.ds(0, size), :], sem.at[m]))
        copies[-1].start()
    low = jnp.int32(0)
    high = jnp.int32(rows * blocks)
    end = jnp.int32(0)
    for s in range(slides):
        end = end + len_ref[s]
        low = jnp.where(end <= me * rows, jnp.maximum(low, end), low)
        high = jnp.where(end >= (me + 1) * rows, jnp.minimum(high, end), high)
    count = jnp.int32(0)
    for m in range(blocks):
        other = jnp.bitwise_xor(me, m) * rows
        before_ref[m] = count
        list_ref[count] = jnp.int32(m)
        count = count + ((other < high) & (other + rows > low)).astype(I32)
    before_ref[blocks] = count
    out_ref[...] = jnp.zeros_like(out_ref)
    lane = lax.broadcasted_iota(I32, (1, LANES), 1)
    outside = jnp.zeros((1, LANES), jnp.bool_)
    for side in range(2):
        outside = outside | ((lane >= S_AT[side]) & (lane < S_AT[side] + slides))
    nothing = jnp.where(outside, -FAR, 0.0)
    for copy in copies:
        copy.wait()
    factor = math.log2(math.e) / math.sqrt(HEAD_DIM)

    def head_step(h, carry):
        entry = HEAD_AT + h * FIELDS
        units = meta_ref[entry + UNITS]
        first = meta_ref[entry + FIRST]
        off = meta_ref[entry + OFFSET]
        some = before_ref[meta_ref[entry + REACH]]
        pair = h >> 1
        side = h & 1

        def attend(u, steps):
            size = u * per
            tile = min(size * 8, rows)
            group = tile // size
            parts = some * steps
            tiles = (parts + (group - 1)) >> (group.bit_length() - 1)
            ours = (lane >= HALF) == (side == 1)

            def take(i, carry):
                block = lax.shift_right_logical(i, steps - 1)
                at = off + (i & (steps - 1)) * size
                keys_ref[pl.ds(pl.multiple_of(i * size, size), size), :] = kvs_ref[
                    list_ref[block], pl.ds(pl.multiple_of(at, per), size), :
                ]
                return carry

            def fill(i, carry):
                keys_ref[pl.ds(pl.multiple_of(i * size, size), size), :] = jnp.broadcast_to(
                    nothing, (size, LANES)
                ).astype(BF16)
                return carry

            lax.fori_loop(0, parts, take, 0)
            lax.fori_loop(parts, tiles * group, fill, 0)

            def q_step(i, carry):
                here = pl.ds(pl.multiple_of(first + i * size, per), size)
                q = q_ref[h, here, :]
                acc_ref[0:size, :] = jnp.zeros((size, LANES), F32)

                def k_step(t, carry):
                    kv = keys_ref[pl.ds(pl.multiple_of(t * tile, tile), tile), :]
                    e = jnp.exp2(dot(q, kv, ((1,), (1,))) * factor)
                    acc_ref[0:size, :] += dot(e.astype(BF16), kv)
                    return carry

                lax.fori_loop(0, tiles, k_step, 0)
                acc = acc_ref[0:size, :]
                total = acc[:, ONE_AT : ONE_AT + 1]
                safe = jnp.where(total > 0, total, 1.0)
                res = jnp.where(total > 0, acc / safe, 0.0).astype(BF16)
                out_ref[pair, here, :] = jnp.where(ours, res, out_ref[pair, here, :])
                return carry

            lax.fori_loop(0, steps, q_step, 0)

        for u in (1, 2, 4):
            pl.when(units == u)(functools.partial(attend, u, jnp.int32(1)))
        pl.when(units >= 8)(functools.partial(attend, 8, units >> 3))
        return carry

    lax.fori_loop(0, heads, head_step, 0)


def away_kernel(slides, len_ref, tok_sums_ref, out_ref, wide_ref, terms_ref, sums_ref):
    pairs, rows, _ = out_ref.shape
    width = wide_ref.shape[1]
    cols = terms_ref.shape[1]
    half = lax.axis_index("head")
    my_start = lax.axis_index(("ctx", "sub")) * rows
    tok = lax.broadcasted_iota(I32, (1, rows), 1)
    per = rows // RES
    tok = my_start + RES * (tok & (per - 1)) + rev_traced(tok // per)
    member = members(len_ref, tok, slides)
    if cols == width:
        columns = slice(None)
        own = jnp.broadcast_to(half == 0, (1, width))
    else:
        columns = pl.ds(pl.multiple_of((1 - half) * cols, LANES), cols)
        lane = lax.broadcasted_iota(I32, (1, width), 1)
        own = (lane >= half * cols) & (lane < half * cols + cols)
    sums = jnp.where(own, tok_sums_ref[:, :width], 0.0)
    for pair in range(pairs):
        pooled = dot(member, out_ref[pair])
        top = pooled.astype(BF16)
        rest = (pooled - top.astype(F32)).astype(BF16)
        both = dot(jnp.concatenate([top, rest], axis=0), wide_ref[pair * LANES : (pair + 1) * LANES, :])
        sums = sums + both[:slides] + both[slides:]
    sums_ref[:, :width] = sums
    sums_ref[:, width:] = tok_sums_ref[:, width:]
    out = jnp.concatenate([out_ref[pair] for pair in range(pairs)], axis=1)
    terms_ref[...] = dot(out, wide_ref[:, columns]).astype(BF16)


def mix_kernel(x_ref, out_ref, wide_ref, got_ref, mixed_ref, p_ref):
    pairs, rows, _ = out_ref.shape
    per = rows // RES
    cols = got_ref.shape[1]
    mine = pl.multiple_of(lax.axis_index("head") * cols, LANES)
    out = jnp.concatenate([out_ref[pair] for pair in range(pairs)], axis=1)
    acc = got_ref[...].astype(F32) + dot(out, wide_ref[:, pl.ds(mine, cols)])
    for c in range(cols // LANES):
        lanes = slice(c * LANES, (c + 1) * LANES)
        for r in range(RES):
            at = rev(r) * per
            p_ref[c, pl.ds(r, per, stride=RES), :] = acc[at : at + per, lanes]
        x = x_ref[:, pl.ds(pl.multiple_of(mine + c * LANES, LANES), LANES)]
        mixed_ref[:, lanes] = (x.astype(F32) + p_ref[c]).astype(BF16)


def loss_kernel(swapped, len_ref, pairs_ref, scale_ref, sums_ref, other_ref, *rest):
    reps, (sim_ref, loss_ref) = rest[:-2], rest[-2:]
    slides = sums_ref.shape[0]
    bank, cols = reps[0].shape
    width = sums_ref.shape[1] - bank
    row = lax.broadcasted_iota(I32, (slides, 1), 0)
    count = jnp.zeros((slides, 1), I32)
    pick = jnp.zeros((slides, 1), I32)
    for s in range(slides):
        count = jnp.where(row == s, len_ref[s], count)
        pick = jnp.where(row == s, pairs_ref[s], pick)
    dots = jnp.zeros((slides, bank), F32)
    ss = jnp.zeros((slides, 1), F32)
    for i, rep in enumerate(reps):
        at = pl.ds(0, cols)
        if swapped:
            half = lax.axis_index("head")
            at = pl.ds(pl.multiple_of((half if i == 0 else 1 - half) * cols, LANES), cols)
        sums = sums_ref[:, at]
        if swapped:
            sums = sums + other_ref[:, at]
        pooled = sums / count.astype(F32)
        ss = ss + jnp.sum(pooled * pooled, axis=1, keepdims=True)
        pieces = []
        left = pooled
        for _ in range(3):
            pieces.append(left.astype(BF16))
            left = left - pieces[-1].astype(F32)
        both = dot(jnp.concatenate(pieces, axis=0), rep[...], ((1,), (1,)))
        dots = dots + both[:slides] + both[slides : 2 * slides] + both[2 * slides :]
    rr = sums_ref[:, width:]
    if swapped:
        rr = rr + other_ref[:, width:]
    scale = jnp.exp(jnp.full((1, 1), scale_ref[0], F32))
    sim = scale * dots / jnp.sqrt((ss + 1e-06) * (rr + 1e-06))
    sim_ref[...] = sim
    total = jnp.sum(jnp.exp(sim - scale), axis=1, keepdims=True)
    lane = lax.broadcasted_iota(I32, (slides, bank), 1)
    picked = jnp.sum(jnp.where(lane == pick, sim, 0.0), axis=1, keepdims=True)
    loss = scale + jnp.log(total) - picked
    here = lax.broadcasted_iota(I32, (slides, slides), 0) == lax.broadcasted_iota(I32, (slides, slides), 1)
    loss_ref[...] = jnp.sum(jnp.where(here, loss, 0.0), axis=0)


SMEM = pl.BlockSpec(memory_space=pltpu.SMEM)
VMEM = pl.BlockSpec(memory_space=pltpu.VMEM)
ANY = pl.BlockSpec(memory_space=pl.ANY)


def call(kernel, out_shape, in_specs, out_specs, scratch=(), grid=(), vmem=16, flops=1000000, moved=1000000):
    return pl.pallas_call(
        kernel,
        grid=grid,
        out_shape=out_shape,
        in_specs=in_specs,
        out_specs=out_specs,
        scratch_shapes=list(scratch),
        compiler_params=pltpu.CompilerParams(vmem_limit_bytes=vmem * MIB),
        cost_estimate=pl.CostEstimate(flops=flops, bytes_accessed=moved, transcendentals=0),
    )


def ladder_of(full):
    steps = ((64, 24, 8), (64, 32, 12), (64, 24, 16), (64, 40, 16), (64, 32, 24), (96, 48, 24), (96, 48, 32), (96, 64, 40))
    fitting = tuple(step for step in steps if step[0] < full)
    return fitting + ((full, full, full),)


def plane(w3, which):
    return pl.BlockSpec((1,) + w3.shape[1:], lambda i: (which, 0, 0))


def run_device(
    tokens, norm_gain, w_qkv, q_gain, k_gain, w_out, seg_len, dilation, slide_len, reports, pairs, log_scale
):
    rows, width = tokens.shape
    feat = w_qkv.shape[2]
    heads = feat // HEAD_DIM
    slides = slide_len.shape[0]
    per = rows // RES
    nz, ns, nx = lax.axis_size("ctx"), lax.axis_size("sub"), lax.axis_size("head")
    blocks = nz * ns
    classes = blocks.bit_length() - 1
    full = heads * RES
    ladder = ladder_of(full)
    cols = width // nx
    swap = [(0, 1), (1, 0)]

    w3 = jnp.transpose(w_qkv, (1, 0, 2))
    pack, normed, meta = call(
        functools.partial(keys_kernel, ladder, heads, nx, classes, slides),
        (
            jax.ShapeDtypeStruct((full * per, LANES), BF16),
            jax.ShapeDtypeStruct((rows, width), BF16),
            jax.ShapeDtypeStruct((HEAD_AT + heads * FIELDS,), I32),
        ),
        [SMEM, SMEM, SMEM, VMEM, VMEM, plane(w3, 1), plane(w3, 2), VMEM],
        (VMEM, VMEM, SMEM),
        [pltpu.VMEM((width // LANES, rows, LANES), F32), pltpu.VMEM((heads, rows, LANES), BF16)],
        grid=(1,),
    )(seg_len, dilation, slide_len, tokens, norm_gain, w3, w3, k_gain)

    bank = reports.shape[0]

    def branch(caps):
        near, mid, far = (min(c, full) * per for c in caps)

        def run(operands):
            pack, normed, tokens, w3, q_gain, w_out, reports, meta, slide_len = operands
            got = {0: pack}
            for m in range(1, nz):
                ends = [(i, i ^ m) for i in range(nz) if abs(i - (i ^ m)) <= nz // 2]
                got[2 * m] = lax.ppermute(pack[: mid if m == 1 else far], "ctx", ends)
            got[1] = lax.ppermute(pack[:near], "sub", swap)
            if nx == 2:
                rep_got = lax.ppermute(reports, "head", swap)
            else:
                rep_got = lax.all_gather(reports, "head", axis=1, tiled=True)
            q, tok_sums, wide = call(
                functools.partial(queries_kernel, heads, slides, blocks),
                (
                    jax.ShapeDtypeStruct((heads, rows, LANES), BF16),
                    jax.ShapeDtypeStruct((slides, width + bank), F32),
                    jax.ShapeDtypeStruct((heads // 2 * LANES, width), BF16),
                ),
                [SMEM, VMEM, VMEM, plane(w3, 0), VMEM, VMEM, VMEM],
                (VMEM, VMEM, VMEM),
                grid=(1,),
                flops=10**9,
                moved=4 * 10**6,
            )(slide_len, tokens, normed, w3, q_gain, w_out, reports)
            for m in range(1, nz):
                got[2 * m + 1] = lax.ppermute(got[2 * m], "sub", swap)
            refs = [got[m] for m in range(blocks)]
            out = call(
                functools.partial(attend_kernel, heads, blocks, slides),
                jax.ShapeDtypeStruct((heads // 2, rows, LANES), BF16),
                [SMEM, SMEM, VMEM] + [ANY] * blocks,
                VMEM,
                [
                    pltpu.VMEM((blocks, full * per, LANES), BF16),
                    pltpu.VMEM((blocks * rows, LANES), BF16),
                    pltpu.VMEM((rows, LANES), F32),
                    pltpu.SMEM((blocks + 1,), I32),
                    pltpu.SMEM((blocks + 1,), I32),
                    pltpu.SemaphoreType.DMA((blocks,)),
                ],
                vmem=6 + (blocks + 2) * full * per * LANES * 2 // MIB,
            )(meta, slide_len, q, *refs)
            return out, tok_sums, wide, rep_got

        return run

    out, tok_sums, wide, rep_got = lax.switch(
        meta[0],
        [branch(caps) for caps in ladder],
        (pack, normed, tokens, w3, q_gain, w_out, reports, meta, slide_len),
    )
    terms, sums = call(
        functools.partial(away_kernel, slides),
        (
            jax.ShapeDtypeStruct((rows, cols if nx == 2 else width), BF16),
            jax.ShapeDtypeStruct((slides, width + bank), F32),
        ),
        [SMEM, VMEM, VMEM, VMEM],
        (VMEM, VMEM),
    )(slide_len, tok_sums, out, wide)
    if nx == 2:
        sums = sums + lax.ppermute(sums, "sub", swap)
        step = 1
        while step < nz:
            sums = sums + lax.ppermute(sums, "ctx", [(i, i ^ step) for i in range(nz)])
            step *= 2
        got = lax.ppermute(terms, "head", swap)
        other = lax.ppermute(sums, "head", swap)
        mixed = call(
            mix_kernel,
            jax.ShapeDtypeStruct((rows, cols), BF16),
            [VMEM] * 4,
            VMEM,
            [pltpu.VMEM((cols // LANES, rows, LANES), F32)],
            flops=10**9,
            moved=4 * 10**6,
        )(tokens, out, wide, got)
        reps = (reports, rep_got)
    else:
        sums = lax.psum(sums, ("ctx", "sub", "head"))
        other = sums
        back = jnp.array([rev(r) for r in range(RES)])
        terms = jnp.transpose(terms.reshape(RES, per, width)[back], (1, 0, 2)).reshape(rows, width)
        proj = lax.psum_scatter(terms, "head", scatter_dimension=1, tiled=True)
        x_cols = lax.dynamic_slice_in_dim(tokens, lax.axis_index("head") * cols, cols, 1)
        mixed = (x_cols.astype(F32) + proj.astype(F32)).astype(BF16)
        reps = (rep_got,)
    similarity, loss = call(
        functools.partial(loss_kernel, nx == 2),
        (jax.ShapeDtypeStruct((slides, bank), F32), jax.ShapeDtypeStruct((slides,), F32)),
        [SMEM, SMEM, SMEM, VMEM, VMEM] + [VMEM] * len(reps),
        (VMEM, VMEM),
    )(slide_len, pairs, log_scale, sums, other, *reps)
    return (mixed, similarity, loss)


def solution(mesh):
    in_specs = (
        P(("groups", "ctx", "sub"), None),
        P(),
        P(None, None, "head"),
        P("head"),
        P("head"),
        P("head", None),
        P(),
        P(),
        P("groups"),
        P(None, "head"),
        P("groups"),
        P(),
    )
    out_specs = (P(("groups", "ctx", "sub"), "head"), P("groups", None), P("groups"))
    return jax.shard_map(run_device, mesh=mesh, in_specs=in_specs, out_specs=out_specs, check_vma=False)
```

```python
import functools
import math

import jax
import jax.numpy as jnp
from jax import lax
from jax.experimental import pallas as pl
from jax.experimental.pallas import tpu as pltpu
from jax.sharding import PartitionSpec as P


HEAD_DIM = 48
RES = 16
LANES = 128
HALF = 64
FAR = 4096.0
MIB = 1024 * 1024
F32 = jnp.float32
BF16 = jnp.bfloat16
I32 = jnp.int32


def rev(r):
    return int(f"{r:04b}"[::-1], 2)


def rev_traced(c):
    return ((c & 1) << 3) | ((c & 2) << 1) | ((c >> 1) & 2) | ((c >> 3) & 1)


def dot(a, b, dims=((1,), (0,)), precision=None):
    return lax.dot_general(a, b, (dims, ((), ())), precision=precision, preferred_element_type=F32)


def units_of(dil_ref, h):
    rate = dil_ref[h]
    count = jnp.int32(RES)
    for step in range(1, RES.bit_length()):
        count = jnp.where(rate == 1 << step, RES >> step, count)
    return count


def first_unit(dil_ref, h):
    return rev_traced(jnp.bitwise_and(h, dil_ref[h] - 1))


UNITS, FIRST, OFFSET, REACH, FIELDS = 0, 1, 2, 3, 4
HEAD_AT = 4


def slide_tiles(len_ref, rows, my_start, slides, one, inside, outside):
    per = rows // RES
    base = RES * lax.broadcasted_iota(I32, (per, LANES), 0) + my_start
    lane = lax.broadcasted_iota(I32, (1, LANES), 1)
    tiles = []
    for side in range(2):
        low, high, on = slide_lanes(len_ref, S_AT[side], slides)
        high = jnp.where(on, high, -1)
        other = jnp.where(on, outside, jnp.where(lane == ONE_AT, one, 0.0))
        parts = []
        for u in range(RES):
            tok = base + rev(u)
            parts.append(jnp.where((tok >= low) & (tok < high), inside, other))
        tiles.append(jnp.concatenate(parts, axis=0))
    return tiles


def slide_lanes(ends_ref, base, slides):
    lane = lax.broadcasted_iota(I32, (1, LANES), 1) - base
    low = jnp.zeros((1, LANES), I32)
    high = jnp.zeros((1, LANES), I32)
    end = jnp.int32(0)
    for s in range(slides):
        low = jnp.where(lane == s, end, low)
        end = end + ends_ref[s]
        high = jnp.where(lane == s, end, high)
    return low, high, (lane >= 0) & (lane < slides)


def selector(source, first, heads_at, target):
    lane = lax.broadcasted_iota(I32, (1, 2 * LANES), 1)
    wanted = jnp.full((1, 2 * LANES), -1, I32)
    for side in range(2):
        at = side * LANES + target[side]
        inside = (lane >= at) & (lane < at + HEAD_DIM)
        wanted = jnp.where(inside, (heads_at + side) * HEAD_DIM - first + lane - at, wanted)
    row = lax.broadcasted_iota(I32, (source, 2 * LANES), 0)
    return jnp.where(row == wanted, 1.0, 0.0).astype(BF16)


V_AT = (0, HALF)
K_AT = (HALF, 0)
S_AT = (HALF + HEAD_DIM, HEAD_DIM)
ONE_AT = HALF - 1


def head_scale(values, feat):
    sq = values * values
    high = sq.astype(BF16)
    low = (sq - high.astype(F32)).astype(BF16)
    lane = lax.broadcasted_iota(I32, (1, feat), 1)
    first = jnp.zeros((1, feat), I32)
    for h in range(1, feat // HEAD_DIM):
        first = jnp.where(lane >= h * HEAD_DIM, h * HEAD_DIM, first)
    row = lax.broadcasted_iota(I32, (feat, feat), 0)
    same = jnp.where((row >= first) & (row < first + HEAD_DIM), 1.0, 0.0).astype(BF16)
    if feat % LANES:
        total = dot(high, same) + dot(low, same)
    else:
        total = dot(jnp.concatenate([high, low], axis=1), jnp.concatenate([same, same], axis=0))
    return lax.rsqrt(total * (1.0 / HEAD_DIM) + 1e-06)


def span(pair, feat):
    first = pair * 2 * HEAD_DIM // LANES * LANES
    last = ((pair + 1) * 2 * HEAD_DIM - 1) // LANES * LANES + LANES
    return first, min(last, feat) - first


def members(slide_ref, tok, slides):
    row = lax.broadcasted_iota(I32, (slides, 1), 0)
    low = jnp.zeros((slides, 1), I32)
    high = jnp.zeros((slides, 1), I32)
    end = jnp.int32(0)
    for s in range(slides):
        low = jnp.where(row == s, end, low)
        end = end + slide_ref[s]
        high = jnp.where(row == s, end, high)
    return jnp.where((tok >= low) & (tok < high), 1.0, 0.0).astype(BF16)


def keys_kernel(
    ladder, heads, parts, classes, slides, seg_hbm, dil_hbm, len_hbm, x_hbm, ng_hbm, w_hbm, kg_hbm,
    pack_ref, normed_ref, meta_ref, xs_ref, kv_ref, x_ref, kv_w_ref, seg_ref, dil_ref, len_ref, ng_ref, kg_ref, sem,
):
    rows, width = x_ref.shape
    feat = heads * HEAD_DIM
    joined = len(kv_w_ref.shape) == 2
    k_w_ref = kv_w_ref.at[:, pl.ds(0, feat)] if joined else kv_w_ref.at[0]
    v_w_ref = kv_w_ref.at[:, pl.ds(feat, feat)] if joined else kv_w_ref.at[1]
    small = []
    for i, (source, target) in enumerate(
        ((seg_hbm, seg_ref), (dil_hbm, dil_ref), (len_hbm, len_ref), (ng_hbm, ng_ref), (kg_hbm, kg_ref))
    ):
        small.append(pltpu.make_async_copy(source, target, sem.at[3 + i]))
        small[-1].start()
    x_copy = pltpu.make_async_copy(x_hbm, x_ref, sem.at[0])
    x_copy.start()
    k_copy = pltpu.make_async_copy(w_hbm.at[1], k_w_ref, sem.at[1])
    k_copy.start()
    v_copy = pltpu.make_async_copy(w_hbm.at[2], v_w_ref, sem.at[2])
    v_copy.start()
    for copy in small:
        copy.wait()
    feat = heads * HEAD_DIM
    per = rows // RES
    base = lax.axis_index("head") * heads
    my_start = lax.axis_index(("ctx", "sub")) * rows
    segs = [seg_ref[h] for h in range(parts * heads)]
    counts = [units_of(dil_ref, h) for h in range(parts * heads)]
    fits = [jnp.bool_(True) for _ in ladder]
    for c in range(1, classes + 1):
        most = jnp.int32(0)
        for part in range(parts):
            total = jnp.int32(0)
            for h in range(part * heads, (part + 1) * heads):
                total = total + jnp.where(segs[h] >= (rows << c), counts[h], 0)
            most = jnp.maximum(most, total)
        for i, caps in enumerate(ladder):
            fits[i] = fits[i] & (most <= caps[min(c, len(caps)) - 1])
    tier = jnp.int32(len(ladder) - 1)
    for i in reversed(range(len(ladder))):
        tier = jnp.where(fits[i], i, tier)
    meta_ref[0] = tier
    local_seg = [seg_ref[base + h] for h in range(heads)]
    local_units = [units_of(dil_ref, base + h) for h in range(heads)]
    starts = [first_unit(dil_ref, base + h) for h in range(heads)]
    offset = []
    for h in range(heads):
        total = jnp.int32(0)
        for other in range(heads):
            ahead = local_seg[other] > local_seg[h]
            if other < h:
                ahead = ahead | (local_seg[other] == local_seg[h])
            if other != h:
                total = total + jnp.where(ahead, local_units[other], 0)
        offset.append(total)
        at = HEAD_AT + h * FIELDS
        meta_ref[at + UNITS] = local_units[h]
        meta_ref[at + FIRST] = starts[h] * per
        meta_ref[at + OFFSET] = total * per
        meta_ref[at + REACH] = local_seg[h] // rows

    x_copy.wait()
    x = x_ref[...].astype(F32)
    mean_sq = jnp.mean(x * x, axis=-1, keepdims=True)
    normal = x * lax.rsqrt(mean_sq + 1e-06) * ng_ref[...].reshape(1, width)
    for c in range(width // LANES):
        lanes = slice(c * LANES, (c + 1) * LANES)
        xs_ref[c] = normal[:, lanes]
        for r in range(RES):
            at = rev(r) * per
            normed_ref[at : at + per, lanes] = xs_ref[c, pl.ds(r, per, stride=RES), :].astype(BF16)
    normed = normed_ref[...]
    k_copy.wait()
    v_copy.wait()
    if joined:
        keys_vals = dot(normed, kv_w_ref[...])
        keys, vals = keys_vals[:, :feat], keys_vals[:, feat:].astype(BF16)
    else:
        keys = dot(normed, kv_w_ref[0])
        vals = dot(normed, kv_w_ref[1]).astype(BF16)
    kn = (keys * head_scale(keys, feat) * kg_ref[...].reshape(1, feat)).astype(BF16)
    extra = slide_tiles(len_ref, rows, my_start, slides, 1.0, 0.0, -FAR)
    for pair in range(heads // 2):
        first, size = span(pair, feat)
        mine = slice(first, first + size)
        to_k, to_v = (selector(size, first, 2 * pair, at) for at in (K_AT, V_AT))
        if feat % LANES:
            both = dot(kn[:, mine], to_k) + dot(vals[:, mine], to_v)
        else:
            both = dot(jnp.concatenate([kn[:, mine], vals[:, mine]], axis=1), jnp.concatenate([to_k, to_v], axis=0))
        for side in range(2):
            h = 2 * pair + side
            kv_ref[h] = (both[:, side * LANES : (side + 1) * LANES] + extra[side]).astype(BF16)

    for h in range(heads):

        def put(u, carry, h=h, to=offset[h], at=starts[h]):
            piece = kv_ref[h, pl.ds(pl.multiple_of((at + u) * per, per), per), :]
            pack_ref[pl.ds(pl.multiple_of((to + u) * per, per), per), :] = piece
            return carry

        lax.fori_loop(0, local_units[h], put, 0)


def queries_kernel(
    heads, slides, blocks, len_ref, x_ref, normed_ref, w_ref, qg_ref, w_out_ref, rep_ref, q_ref, sums_ref, wide_ref
):
    rows = normed_ref.shape[0]
    feat = heads * HEAD_DIM
    my_start = lax.axis_index(("ctx", "sub")) * rows
    piece = rows // 4
    per = rows // RES
    base = RES * lax.broadcasted_iota(I32, (per, LANES), 0) + my_start

    def step(i, carry):
        here = pl.ds(pl.multiple_of(i * piece, piece), piece)
        q = dot(normed_ref[here, :], w_ref[0])
        qn = (q * head_scale(q, feat) * qg_ref[...].reshape(1, feat)).astype(BF16)
        extra = []
        for side in range(2):
            low, high, on = slide_lanes(len_ref, S_AT[side], slides)
            high = jnp.where(on, high, -1)
            parts = []
            for u in range(piece // per):
                tok = base + rev_traced(i * (piece // per) + u)
                parts.append(jnp.where((tok >= low) & (tok < high), 1.0, 0.0))
            extra.append(jnp.concatenate(parts, axis=0))
        for pair in range(heads // 2):
            first, size = span(pair, feat)
            both = dot(qn[:, first : first + size], selector(size, first, 2 * pair, K_AT))
            for side in range(2):
                lanes = slice(side * LANES, (side + 1) * LANES)
                q_ref[2 * pair + side, here, :] = (both[:, lanes] + extra[side]).astype(BF16)
        return carry

    lax.fori_loop(0, rows // piece, step, 0)
    place = lax.broadcasted_iota(I32, (1, rows), 1) + my_start
    width = x_ref.shape[1]
    sums_ref[:, :width] = dot(members(len_ref, place, slides), x_ref[...])
    rep = rep_ref[...].astype(F32)
    share = jnp.full((slides, rep.shape[1]), 1.0 / blocks, F32)
    sums_ref[:, width:] = dot(share, rep * rep, ((1,), (1,)), lax.Precision.HIGHEST)
    wide_ref[...] = jnp.zeros_like(wide_ref)
    for h in range(heads):
        at = h // 2 * LANES + V_AT[h % 2]
        wide_ref[at : at + HEAD_DIM, :] = w_out_ref[h * HEAD_DIM : (h + 1) * HEAD_DIM, :]


def attend_kernel(heads, blocks, begin, slides, meta_ref, len_ref, q_ref, *rest):
    stop = 2 if begin == 0 else blocks
    if begin > 0:
        out_in_ref, acc_in_ref, *rest = rest
    kv_refs, rest = rest[: stop - begin], rest[stop - begin :]
    if begin > 0:
        out_ref, *rest = rest
    else:
        out_ref, acc_out_ref, *rest = rest
    kvs_ref, keys_ref, acc_ref, list_ref, before_ref, sem = rest
    rows = q_ref.shape[1]
    per = rows // RES
    me = lax.axis_index(("ctx", "sub"))
    copies = []
    for i, kv_ref in enumerate(kv_refs):
        size = kv_ref.shape[0]
        copies.append(pltpu.make_async_copy(kv_ref, kvs_ref.at[i, pl.ds(0, size), :], sem.at[i]))
        copies[-1].start()
    low = jnp.int32(0)
    high = jnp.int32(rows * blocks)
    end = jnp.int32(0)
    for s in range(slides):
        end = end + len_ref[s]
        low = jnp.where(end <= me * rows, jnp.maximum(low, end), low)
        high = jnp.where(end >= (me + 1) * rows, jnp.minimum(high, end), high)
    count = jnp.int32(0)
    for i, m in enumerate(range(begin, stop)):
        other = jnp.bitwise_xor(me, m) * rows
        before_ref[i] = count
        list_ref[count] = jnp.int32(i)
        count = count + ((other < high) & (other + rows > low)).astype(I32)
    before_ref[stop - begin] = count
    out_ref[...] = jnp.zeros_like(out_ref) if begin == 0 else out_in_ref[...]
    lane = lax.broadcasted_iota(I32, (1, LANES), 1)
    outside = jnp.zeros((1, LANES), jnp.bool_)
    for side in range(2):
        outside = outside | ((lane >= S_AT[side]) & (lane < S_AT[side] + slides))
    nothing = jnp.where(outside, -FAR, 0.0)
    for copy in copies:
        copy.wait()
    factor = math.log2(math.e) / math.sqrt(HEAD_DIM)

    def head_step(h, carry):
        entry = HEAD_AT + h * FIELDS
        units = meta_ref[entry + UNITS]
        first = meta_ref[entry + FIRST]
        off = meta_ref[entry + OFFSET]
        some = before_ref[jnp.clip(meta_ref[entry + REACH], begin, stop) - begin]
        pair = h >> 1
        side = h & 1

        def attend(u, steps):
            size = u * per
            tile = min(size * min(8, pl.next_power_of_2(stop - begin)), rows)
            group = tile // size
            parts = some * steps
            tiles = (parts + (group - 1)) >> (group.bit_length() - 1)
            ours = (lane >= HALF) == (side == 1)

            def take(i, carry):
                block = lax.shift_right_logical(i, steps - 1)
                at = off + (i & (steps - 1)) * size
                keys_ref[pl.ds(pl.multiple_of(i * size, size), size), :] = kvs_ref[
                    list_ref[block], pl.ds(pl.multiple_of(at, per), size), :
                ]
                return carry

            def fill(i, carry):
                keys_ref[pl.ds(pl.multiple_of(i * size, size), size), :] = jnp.broadcast_to(
                    nothing, (size, LANES)
                ).astype(BF16)
                return carry

            lax.fori_loop(0, parts, take, 0)
            lax.fori_loop(parts, tiles * group, fill, 0)

            def q_step(i, carry):
                here = pl.ds(pl.multiple_of(first + i * size, per), size)
                q = q_ref[h, here, :]
                acc_ref[0:size, :] = jnp.zeros((size, LANES), F32) if begin == 0 else acc_in_ref[h, here, :]

                def k_step(t, carry):
                    kv = keys_ref[pl.ds(pl.multiple_of(t * tile, tile), tile), :]
                    e = jnp.exp2(dot(q, kv, ((1,), (1,))) * factor)
                    acc_ref[0:size, :] += dot(e.astype(BF16), kv)
                    return carry

                lax.fori_loop(0, tiles, k_step, 0)
                acc = acc_ref[0:size, :]
                if begin == 0:
                    acc_out_ref[h, here, :] = acc
                total = acc[:, ONE_AT : ONE_AT + 1]
                safe = jnp.where(total > 0, total, 1.0)
                res = jnp.where(total > 0, acc / safe, 0.0).astype(BF16)
                out_ref[pair, here, :] = jnp.where(ours, res, out_ref[pair, here, :])
                return carry

            lax.fori_loop(0, steps, q_step, 0)

        for u in (1, 2, 4):
            pl.when((units == u) & (some > 0))(functools.partial(attend, u, jnp.int32(1)))
        pl.when((units >= 8) & (some > 0))(functools.partial(attend, 8, units >> 3))
        return carry

    lax.fori_loop(0, heads, head_step, 0)


def away_kernel(slides, len_ref, tok_sums_ref, out_ref, wide_ref, terms_ref, sums_ref):
    pairs, rows, _ = out_ref.shape
    width = wide_ref.shape[1]
    cols = terms_ref.shape[1]
    half = lax.axis_index("head")
    my_start = lax.axis_index(("ctx", "sub")) * rows
    tok = lax.broadcasted_iota(I32, (1, rows), 1)
    per = rows // RES
    tok = my_start + RES * (tok & (per - 1)) + rev_traced(tok // per)
    member = members(len_ref, tok, slides)
    if cols == width:
        columns = slice(None)
        own = jnp.broadcast_to(half == 0, (1, width))
    else:
        columns = pl.ds(pl.multiple_of((1 - half) * cols, LANES), cols)
        lane = lax.broadcasted_iota(I32, (1, width), 1)
        own = (lane >= half * cols) & (lane < half * cols + cols)
    sums = jnp.where(own, tok_sums_ref[:, :width], 0.0)
    for pair in range(pairs):
        pooled = dot(member, out_ref[pair])
        top = pooled.astype(BF16)
        rest = (pooled - top.astype(F32)).astype(BF16)
        both = dot(jnp.concatenate([top, rest], axis=0), wide_ref[pair * LANES : (pair + 1) * LANES, :])
        sums = sums + both[:slides] + both[slides:]
    sums_ref[:, :width] = sums
    sums_ref[:, width:] = tok_sums_ref[:, width:]
    out = jnp.concatenate([out_ref[pair] for pair in range(pairs)], axis=1)
    terms_ref[...] = dot(out, wide_ref[:, columns]).astype(BF16)


def unpermute(values, p_ref):
    rows = values.shape[0]
    per = rows // RES
    for c in range(values.shape[1] // LANES):
        for r in range(RES):
            at = rev(r) * per
            p_ref[c, pl.ds(r, per, stride=RES), :] = values[at : at + per, c * LANES : (c + 1) * LANES]


def own_kernel(x_ref, out_ref, wide_ref, y_ref, p_ref):
    pairs = out_ref.shape[0]
    cols = y_ref.shape[1]
    mine = pl.multiple_of(lax.axis_index("head") * cols, LANES)
    out = jnp.concatenate([out_ref[pair] for pair in range(pairs)], axis=1)
    unpermute(dot(out, wide_ref[:, pl.ds(mine, cols)]), p_ref)
    for c in range(cols // LANES):
        x = x_ref[:, pl.ds(pl.multiple_of(mine + c * LANES, LANES), LANES)]
        y_ref[:, c * LANES : (c + 1) * LANES] = x.astype(F32) + p_ref[c]


def mix_kernel(y_ref, got_ref, mixed_ref, p_ref):
    unpermute(got_ref[...].astype(F32), p_ref)
    for c in range(y_ref.shape[1] // LANES):
        lanes = slice(c * LANES, (c + 1) * LANES)
        mixed_ref[:, lanes] = (y_ref[:, lanes] + p_ref[c]).astype(BF16)


def loss_kernel(swapped, len_ref, pairs_ref, scale_ref, sums_ref, other_ref, *rest):
    reps, (sim_ref, loss_ref) = rest[:-2], rest[-2:]
    slides = sums_ref.shape[0]
    bank, cols = reps[0].shape
    width = sums_ref.shape[1] - bank
    row = lax.broadcasted_iota(I32, (slides, 1), 0)
    count = jnp.zeros((slides, 1), I32)
    pick = jnp.zeros((slides, 1), I32)
    for s in range(slides):
        count = jnp.where(row == s, len_ref[s], count)
        pick = jnp.where(row == s, pairs_ref[s], pick)
    dots = jnp.zeros((slides, bank), F32)
    ss = jnp.zeros((slides, 1), F32)
    for i, rep in enumerate(reps):
        at = pl.ds(0, cols)
        if swapped:
            half = lax.axis_index("head")
            at = pl.ds(pl.multiple_of((half if i == 0 else 1 - half) * cols, LANES), cols)
        sums = sums_ref[:, at]
        if swapped:
            sums = sums + other_ref[:, at]
        pooled = sums / count.astype(F32)
        ss = ss + jnp.sum(pooled * pooled, axis=1, keepdims=True)
        pieces = []
        left = pooled
        for _ in range(3):
            pieces.append(left.astype(BF16))
            left = left - pieces[-1].astype(F32)
        both = dot(jnp.concatenate(pieces, axis=0), rep[...], ((1,), (1,)))
        dots = dots + both[:slides] + both[slides : 2 * slides] + both[2 * slides :]
    rr = sums_ref[:, width:]
    if swapped:
        rr = rr + other_ref[:, width:]
    scale = jnp.exp(jnp.full((1, 1), scale_ref[0], F32))
    sim = scale * dots / jnp.sqrt((ss + 1e-06) * (rr + 1e-06))
    sim_ref[...] = sim
    total = jnp.sum(jnp.exp(sim - scale), axis=1, keepdims=True)
    lane = lax.broadcasted_iota(I32, (slides, bank), 1)
    picked = jnp.sum(jnp.where(lane == pick, sim, 0.0), axis=1, keepdims=True)
    loss = scale + jnp.log(total) - picked
    here = lax.broadcasted_iota(I32, (slides, slides), 0) == lax.broadcasted_iota(I32, (slides, slides), 1)
    loss_ref[...] = jnp.sum(jnp.where(here, loss, 0.0), axis=0)


SMEM = pl.BlockSpec(memory_space=pltpu.SMEM)
VMEM = pl.BlockSpec(memory_space=pltpu.VMEM)
ANY = pl.BlockSpec(memory_space=pl.ANY)
HBM = pl.BlockSpec(memory_space=pltpu.HBM)


def call(kernel, out_shape, in_specs, out_specs, scratch=(), grid=(), vmem=16, flops=1000000, moved=1000000):
    return pl.pallas_call(
        kernel,
        grid=grid,
        out_shape=out_shape,
        in_specs=in_specs,
        out_specs=out_specs,
        scratch_shapes=list(scratch),
        compiler_params=pltpu.CompilerParams(vmem_limit_bytes=vmem * MIB),
        cost_estimate=pl.CostEstimate(flops=flops, bytes_accessed=moved, transcendentals=0),
    )


def ladder_of(full):
    steps = ((96, 38, 18), (96, 42, 21), (96, 50, 25), (96, 58, 29), (96, 68, 34), (96, 82, 41), (96, 82, 58))
    fitting = tuple(step for step in steps if step[0] < full)
    return fitting + ((full, full, full),)


def plane(w3, which):
    return pl.BlockSpec((1,) + w3.shape[1:], lambda i: (which, 0, 0))


def run_device(
    tokens, norm_gain, w_qkv, q_gain, k_gain, w_out, seg_len, dilation, slide_len, reports, pairs, log_scale
):
    rows, width = tokens.shape
    feat = w_qkv.shape[2]
    heads = feat // HEAD_DIM
    slides = slide_len.shape[0]
    per = rows // RES
    nz, ns, nx = lax.axis_size("ctx"), lax.axis_size("sub"), lax.axis_size("head")
    blocks = nz * ns
    classes = blocks.bit_length() - 1
    full = heads * RES
    ladder = ladder_of(full)
    cols = width // nx
    swap = [(0, 1), (1, 0)]

    w3 = jnp.transpose(w_qkv, (1, 0, 2))
    pack, normed, meta = call(
        functools.partial(keys_kernel, ladder, heads, nx, classes, slides),
        (
            jax.ShapeDtypeStruct((full * per, LANES), BF16),
            jax.ShapeDtypeStruct((rows, width), BF16),
            jax.ShapeDtypeStruct((HEAD_AT + heads * FIELDS,), I32),
        ),
        [HBM] * 7,
        (VMEM, VMEM, SMEM),
        [
            pltpu.VMEM((width // LANES, rows, LANES), F32),
            pltpu.VMEM((heads, rows, LANES), BF16),
            pltpu.VMEM((rows, width), BF16),
            pltpu.VMEM((2, width, feat) if feat % LANES else (width, 2 * feat), BF16),
            pltpu.SMEM(seg_len.shape, I32),
            pltpu.SMEM(dilation.shape, I32),
            pltpu.SMEM(slide_len.shape, I32),
            pltpu.VMEM((width,), F32),
            pltpu.VMEM((feat,), F32),
            pltpu.SemaphoreType.DMA((8,)),
        ],
    )(*(pltpu.with_memory_space_constraint(a, pltpu.HBM) for a in (seg_len, dilation, slide_len, tokens, norm_gain, w3, k_gain)))

    bank = reports.shape[0]

    def branch(caps):
        near, mid, far = (min(c, full) * per for c in caps)

        def run(operands):
            pack, normed, tokens, w3, q_gain, w_out, reports, meta, slide_len = operands
            got = {0: pack}
            for m in range(1, nz):
                ends = [(i, i ^ m) for i in range(nz) if abs(i - (i ^ m)) <= nz // 2]
                got[2 * m] = lax.ppermute(pack[: mid if m == 1 else far], "ctx", ends)
            got[1] = lax.ppermute(pack[:near], "sub", swap)
            if nx == 2:
                rep_got = lax.ppermute(reports, "head", swap)
            else:
                rep_got = lax.all_gather(reports, "head", axis=1, tiled=True)
            q, tok_sums, wide = call(
                functools.partial(queries_kernel, heads, slides, blocks),
                (
                    jax.ShapeDtypeStruct((heads, rows, LANES), BF16),
                    jax.ShapeDtypeStruct((slides, width + bank), F32),
                    jax.ShapeDtypeStruct((heads // 2 * LANES, width), BF16),
                ),
                [SMEM, VMEM, VMEM, plane(w3, 0), VMEM, VMEM, VMEM],
                (VMEM, VMEM, VMEM),
                grid=(1,),
                flops=10**9,
                moved=4 * 10**6,
            )(slide_len, tokens, normed, w3, q_gain, w_out, reports)

            def scratch(count):
                return [
                    pltpu.VMEM((count, full * per, LANES), BF16),
                    pltpu.VMEM((pl.next_power_of_2(count) * rows, LANES), BF16),
                    pltpu.VMEM((8 * per, LANES), F32),
                    pltpu.SMEM((count + 1,), I32),
                    pltpu.SMEM((count + 1,), I32),
                    pltpu.SemaphoreType.DMA((count,)),
                ]

            kept = jax.ShapeDtypeStruct((heads // 2, rows, LANES), BF16)
            out, acc = call(
                functools.partial(attend_kernel, heads, blocks, 0, slides),
                (kept, jax.ShapeDtypeStruct((heads, rows, LANES), F32)),
                [SMEM, SMEM, VMEM] + [ANY] * 2,
                (VMEM, VMEM),
                scratch(2),
                flops=10**9,
                moved=8 * 10**6,
            )(meta, slide_len, q, got[0], got[1])
            for m in range(1, nz):
                got[2 * m + 1] = lax.ppermute(got[2 * m], "sub", swap)
            out = call(
                functools.partial(attend_kernel, heads, blocks, 2, slides),
                kept,
                [SMEM, SMEM, VMEM, VMEM, VMEM] + [ANY] * (blocks - 2),
                VMEM,
                scratch(blocks - 2),
                vmem=10 + blocks * full * per * LANES * 2 // MIB + blocks * rows * LANES * 4 // MIB,
            )(meta, slide_len, q, out, acc, *(got[m] for m in range(2, blocks)))
            return out, tok_sums, wide, rep_got

        return run

    out, tok_sums, wide, rep_got = lax.switch(
        meta[0],
        [branch(caps) for caps in ladder],
        (pack, normed, tokens, w3, q_gain, w_out, reports, meta, slide_len),
    )
    terms, sums = call(
        functools.partial(away_kernel, slides),
        (
            jax.ShapeDtypeStruct((rows, cols if nx == 2 else width), BF16),
            jax.ShapeDtypeStruct((slides, width + bank), F32),
        ),
        [SMEM, VMEM, VMEM, VMEM],
        (VMEM, VMEM),
    )(slide_len, tok_sums, out, wide)
    if nx == 2:
        sums = sums + lax.ppermute(sums, "sub", swap)
        step = 1
        while step < nz:
            sums = sums + lax.ppermute(sums, "ctx", [(i, i ^ step) for i in range(nz)])
            step *= 2
        got = lax.ppermute(terms, "head", swap)
        other = lax.ppermute(sums, "head", swap)
        unpermuted = pltpu.VMEM((cols // LANES, rows, LANES), F32)
        y = call(
            own_kernel,
            jax.ShapeDtypeStruct((rows, cols), F32),
            [VMEM] * 3,
            VMEM,
            [unpermuted],
            flops=10**9,
            moved=4 * 10**6,
        )(tokens, out, wide)
        mixed = call(
            mix_kernel,
            jax.ShapeDtypeStruct((rows, cols), BF16),
            [VMEM] * 2,
            VMEM,
            [unpermuted],
            flops=10**8,
            moved=2 * 10**6,
        )(y, got)
        reps = (reports, rep_got)
    else:
        sums = lax.psum(sums, ("ctx", "sub", "head"))
        other = sums
        back = jnp.array([rev(r) for r in range(RES)])
        terms = jnp.transpose(terms.reshape(RES, per, width)[back], (1, 0, 2)).reshape(rows, width)
        proj = lax.psum_scatter(terms, "head", scatter_dimension=1, tiled=True)
        x_cols = lax.dynamic_slice_in_dim(tokens, lax.axis_index("head") * cols, cols, 1)
        mixed = (x_cols.astype(F32) + proj.astype(F32)).astype(BF16)
        reps = (rep_got,)
    similarity, loss = call(
        functools.partial(loss_kernel, nx == 2),
        (jax.ShapeDtypeStruct((slides, bank), F32), jax.ShapeDtypeStruct((slides,), F32)),
        [SMEM, SMEM, SMEM, VMEM, VMEM] + [VMEM] * len(reps),
        (VMEM, VMEM),
    )(slide_len, pairs, log_scale, sums, other, *reps)
    return (mixed, similarity, loss)


def solution(mesh):
    in_specs = (
        P(("groups", "ctx", "sub"), None),
        P(),
        P(None, None, "head"),
        P("head"),
        P("head"),
        P("head", None),
        P(),
        P(),
        P("groups"),
        P(None, "head"),
        P("groups"),
        P(),
    )
    out_specs = (P(("groups", "ctx", "sub"), "head"), P("groups", None), P("groups"))
    return jax.shard_map(run_device, mesh=mesh, in_specs=in_specs, out_specs=out_specs, check_vma=False)
```

```python
import functools
import math

import jax
import jax.numpy as jnp
from jax import lax
from jax.experimental import pallas as pl
from jax.experimental.pallas import tpu as pltpu
from jax.sharding import PartitionSpec as P


HEAD_DIM = 48
RES = 16
LANES = 128
HALF = 64
FAR = 4096.0
MIB = 1024 * 1024
F32 = jnp.float32
BF16 = jnp.bfloat16
I32 = jnp.int32


def rev(r):
    return int(f"{r:04b}"[::-1], 2)


def rev_traced(c):
    return ((c & 1) << 3) | ((c & 2) << 1) | ((c >> 1) & 2) | ((c >> 3) & 1)


def dot(a, b, dims=((1,), (0,)), precision=None):
    return lax.dot_general(a, b, (dims, ((), ())), precision=precision, preferred_element_type=F32)


def units_of(dil_ref, h):
    rate = dil_ref[h]
    count = jnp.int32(RES)
    for step in range(1, RES.bit_length()):
        count = jnp.where(rate == 1 << step, RES >> step, count)
    return count


def first_unit(dil_ref, h):
    return rev_traced(jnp.bitwise_and(h, dil_ref[h] - 1))


UNITS, FIRST, OFFSET, REACH, FIELDS = 0, 1, 2, 3, 4
HEAD_AT = 4


def slide_tiles(len_ref, rows, my_start, slides, one, inside, outside):
    per = rows // RES
    base = RES * lax.broadcasted_iota(I32, (per, LANES), 0) + my_start
    lane = lax.broadcasted_iota(I32, (1, LANES), 1)
    tiles = []
    for side in range(2):
        low, high, on = slide_lanes(len_ref, S_AT[side], slides)
        high = jnp.where(on, high, -1)
        other = jnp.where(on, outside, jnp.where(lane == ONE_AT, one, 0.0))
        parts = []
        for u in range(RES):
            tok = base + rev(u)
            parts.append(jnp.where((tok >= low) & (tok < high), inside, other))
        tiles.append(jnp.concatenate(parts, axis=0))
    return tiles


def slide_lanes(ends_ref, base, slides):
    lane = lax.broadcasted_iota(I32, (1, LANES), 1) - base
    low = jnp.zeros((1, LANES), I32)
    high = jnp.zeros((1, LANES), I32)
    end = jnp.int32(0)
    for s in range(slides):
        low = jnp.where(lane == s, end, low)
        end = end + ends_ref[s]
        high = jnp.where(lane == s, end, high)
    return low, high, (lane >= 0) & (lane < slides)


def selector(source, first, heads_at, target):
    lane = lax.broadcasted_iota(I32, (1, 2 * LANES), 1)
    wanted = jnp.full((1, 2 * LANES), -1, I32)
    for side in range(2):
        at = side * LANES + target[side]
        inside = (lane >= at) & (lane < at + HEAD_DIM)
        wanted = jnp.where(inside, (heads_at + side) * HEAD_DIM - first + lane - at, wanted)
    row = lax.broadcasted_iota(I32, (source, 2 * LANES), 0)
    return jnp.where(row == wanted, 1.0, 0.0).astype(BF16)


V_AT = (0, HALF)
K_AT = (HALF, 0)
S_AT = (HALF + HEAD_DIM, HEAD_DIM)
ONE_AT = HALF - 1


def head_scale(values, feat):
    sq = values * values
    high = sq.astype(BF16)
    low = (sq - high.astype(F32)).astype(BF16)
    lane = lax.broadcasted_iota(I32, (1, feat), 1)
    first = jnp.zeros((1, feat), I32)
    for h in range(1, feat // HEAD_DIM):
        first = jnp.where(lane >= h * HEAD_DIM, h * HEAD_DIM, first)
    row = lax.broadcasted_iota(I32, (feat, feat), 0)
    same = jnp.where((row >= first) & (row < first + HEAD_DIM), 1.0, 0.0).astype(BF16)
    if feat % LANES:
        total = dot(high, same) + dot(low, same)
    else:
        total = dot(jnp.concatenate([high, low], axis=1), jnp.concatenate([same, same], axis=0))
    return lax.rsqrt(total * (1.0 / HEAD_DIM) + 1e-06)


def span(pair, feat):
    first = pair * 2 * HEAD_DIM // LANES * LANES
    last = ((pair + 1) * 2 * HEAD_DIM - 1) // LANES * LANES + LANES
    return first, min(last, feat) - first


def members(slide_ref, tok, slides):
    row = lax.broadcasted_iota(I32, (slides, 1), 0)
    low = jnp.zeros((slides, 1), I32)
    high = jnp.zeros((slides, 1), I32)
    end = jnp.int32(0)
    for s in range(slides):
        low = jnp.where(row == s, end, low)
        end = end + slide_ref[s]
        high = jnp.where(row == s, end, high)
    return jnp.where((tok >= low) & (tok < high), 1.0, 0.0).astype(BF16)


def keys_kernel(
    ladder, heads, parts, classes, slides, seg_hbm, dil_hbm, len_hbm, x_hbm, ng_hbm, w_hbm, kg_hbm,
    pack_ref, normed_ref, meta_ref, xs_ref, kv_ref, x_ref, kv_w_ref, seg_ref, dil_ref, len_ref, ng_ref, kg_ref, sem,
):
    rows, width = x_ref.shape
    feat = heads * HEAD_DIM
    joined = len(kv_w_ref.shape) == 2
    k_w_ref = kv_w_ref.at[:, pl.ds(0, feat)] if joined else kv_w_ref.at[0]
    v_w_ref = kv_w_ref.at[:, pl.ds(feat, feat)] if joined else kv_w_ref.at[1]
    small = []
    for i, (source, target) in enumerate(
        ((seg_hbm, seg_ref), (dil_hbm, dil_ref), (len_hbm, len_ref), (ng_hbm, ng_ref), (kg_hbm, kg_ref))
    ):
        small.append(pltpu.make_async_copy(source, target, sem.at[3 + i]))
        small[-1].start()
    x_copy = pltpu.make_async_copy(x_hbm, x_ref, sem.at[0])
    x_copy.start()
    k_copy = pltpu.make_async_copy(w_hbm.at[1], k_w_ref, sem.at[1])
    k_copy.start()
    v_copy = pltpu.make_async_copy(w_hbm.at[2], v_w_ref, sem.at[2])
    v_copy.start()
    for copy in small:
        copy.wait()
    feat = heads * HEAD_DIM
    per = rows // RES
    base = lax.axis_index("head") * heads
    my_start = lax.axis_index(("ctx", "sub")) * rows
    segs = [seg_ref[h] for h in range(parts * heads)]
    counts = [units_of(dil_ref, h) for h in range(parts * heads)]
    fits = [jnp.bool_(True) for _ in ladder]
    for c in range(1, classes + 1):
        most = jnp.int32(0)
        for part in range(parts):
            total = jnp.int32(0)
            for h in range(part * heads, (part + 1) * heads):
                total = total + jnp.where(segs[h] >= (rows << c), counts[h], 0)
            most = jnp.maximum(most, total)
        for i, caps in enumerate(ladder):
            fits[i] = fits[i] & (most <= caps[min(c, len(caps)) - 1])
    tier = jnp.int32(len(ladder) - 1)
    for i in reversed(range(len(ladder))):
        tier = jnp.where(fits[i], i, tier)
    meta_ref[0] = tier
    local_seg = [seg_ref[base + h] for h in range(heads)]
    local_units = [units_of(dil_ref, base + h) for h in range(heads)]
    starts = [first_unit(dil_ref, base + h) for h in range(heads)]
    offset = []
    for h in range(heads):
        total = jnp.int32(0)
        for other in range(heads):
            ahead = local_seg[other] > local_seg[h]
            if other < h:
                ahead = ahead | (local_seg[other] == local_seg[h])
            if other != h:
                total = total + jnp.where(ahead, local_units[other], 0)
        offset.append(total)
        at = HEAD_AT + h * FIELDS
        meta_ref[at + UNITS] = local_units[h]
        meta_ref[at + FIRST] = starts[h] * per
        meta_ref[at + OFFSET] = total * per
        meta_ref[at + REACH] = local_seg[h] // rows

    x_copy.wait()
    x = x_ref[...].astype(F32)
    mean_sq = jnp.mean(x * x, axis=-1, keepdims=True)
    normal = x * lax.rsqrt(mean_sq + 1e-06) * ng_ref[...].reshape(1, width)
    for c in range(width // LANES):
        lanes = slice(c * LANES, (c + 1) * LANES)
        xs_ref[c] = normal[:, lanes]
        for r in range(RES):
            at = rev(r) * per
            normed_ref[at : at + per, lanes] = xs_ref[c, pl.ds(r, per, stride=RES), :].astype(BF16)
    normed = normed_ref[...]
    k_copy.wait()
    v_copy.wait()
    if joined:
        keys_vals = dot(normed, kv_w_ref[...])
        keys, vals = keys_vals[:, :feat], keys_vals[:, feat:].astype(BF16)
    else:
        keys = dot(normed, kv_w_ref[0])
        vals = dot(normed, kv_w_ref[1]).astype(BF16)
    kn = (keys * head_scale(keys, feat) * kg_ref[...].reshape(1, feat)).astype(BF16)
    extra = slide_tiles(len_ref, rows, my_start, slides, 1.0, 0.0, -FAR)
    for pair in range(heads // 2):
        first, size = span(pair, feat)
        mine = slice(first, first + size)
        to_k, to_v = (selector(size, first, 2 * pair, at) for at in (K_AT, V_AT))
        if feat % LANES:
            both = dot(kn[:, mine], to_k) + dot(vals[:, mine], to_v)
        else:
            both = dot(jnp.concatenate([kn[:, mine], vals[:, mine]], axis=1), jnp.concatenate([to_k, to_v], axis=0))
        for side in range(2):
            h = 2 * pair + side
            kv_ref[h] = (both[:, side * LANES : (side + 1) * LANES] + extra[side]).astype(BF16)

    for h in range(heads):

        def put(u, carry, h=h, to=offset[h], at=starts[h]):
            piece = kv_ref[h, pl.ds(pl.multiple_of((at + u) * per, per), per), :]
            pack_ref[pl.ds(pl.multiple_of((to + u) * per, per), per), :] = piece
            return carry

        lax.fori_loop(0, local_units[h], put, 0)


def queries_kernel(
    heads, slides, blocks, len_ref, x_ref, normed_ref, w_ref, qg_ref, w_out_ref, rep_ref, q_ref, sums_ref, wide_ref
):
    rows = normed_ref.shape[0]
    feat = heads * HEAD_DIM
    my_start = lax.axis_index(("ctx", "sub")) * rows
    piece = rows // 4
    per = rows // RES
    base = RES * lax.broadcasted_iota(I32, (per, LANES), 0) + my_start

    def step(i, carry):
        here = pl.ds(pl.multiple_of(i * piece, piece), piece)
        q = dot(normed_ref[here, :], w_ref[0])
        qn = (q * head_scale(q, feat) * qg_ref[...].reshape(1, feat)).astype(BF16)
        extra = []
        for side in range(2):
            low, high, on = slide_lanes(len_ref, S_AT[side], slides)
            high = jnp.where(on, high, -1)
            parts = []
            for u in range(piece // per):
                tok = base + rev_traced(i * (piece // per) + u)
                parts.append(jnp.where((tok >= low) & (tok < high), 1.0, 0.0))
            extra.append(jnp.concatenate(parts, axis=0))
        for pair in range(heads // 2):
            first, size = span(pair, feat)
            both = dot(qn[:, first : first + size], selector(size, first, 2 * pair, K_AT))
            for side in range(2):
                lanes = slice(side * LANES, (side + 1) * LANES)
                q_ref[2 * pair + side, here, :] = (both[:, lanes] + extra[side]).astype(BF16)
        return carry

    lax.fori_loop(0, rows // piece, step, 0)
    place = lax.broadcasted_iota(I32, (1, rows), 1) + my_start
    width = x_ref.shape[1]
    sums_ref[:, :width] = dot(members(len_ref, place, slides), x_ref[...])
    rep = rep_ref[...].astype(F32)
    share = jnp.full((slides, rep.shape[1]), 1.0 / blocks, F32)
    sums_ref[:, width:] = dot(share, rep * rep, ((1,), (1,)), lax.Precision.HIGHEST)
    wide_ref[...] = jnp.zeros_like(wide_ref)
    for h in range(heads):
        at = h // 2 * LANES + V_AT[h % 2]
        wide_ref[at : at + HEAD_DIM, :] = w_out_ref[h * HEAD_DIM : (h + 1) * HEAD_DIM, :]


def attend_kernel(heads, blocks, begin, slides, meta_ref, len_ref, q_ref, *rest):
    stop = 2 if begin == 0 else blocks
    if begin > 0:
        out_in_ref, acc_in_ref, *rest = rest
    kv_refs, rest = rest[: stop - begin], rest[stop - begin :]
    if begin > 0:
        out_ref, *rest = rest
    else:
        out_ref, acc_out_ref, *rest = rest
    keys_ref, acc_ref, before_ref = rest
    rows = q_ref.shape[1]
    per = rows // RES
    me = lax.axis_index(("ctx", "sub"))
    low = jnp.int32(0)
    high = jnp.int32(rows * blocks)
    end = jnp.int32(0)
    for s in range(slides):
        end = end + len_ref[s]
        low = jnp.where(end <= me * rows, jnp.maximum(low, end), low)
        high = jnp.where(end >= (me + 1) * rows, jnp.minimum(high, end), high)
    count = jnp.int32(0)
    for i, m in enumerate(range(begin, stop)):
        other = jnp.bitwise_xor(me, m) * rows
        before_ref[i] = count
        count = count + ((other < high) & (other + rows > low)).astype(I32)
    before_ref[stop - begin] = count
    out_ref[...] = jnp.zeros_like(out_ref) if begin == 0 else out_in_ref[...]
    lane = lax.broadcasted_iota(I32, (1, LANES), 1)
    outside = jnp.zeros((1, LANES), jnp.bool_)
    for side in range(2):
        outside = outside | ((lane >= S_AT[side]) & (lane < S_AT[side] + slides))
    nothing = jnp.where(outside, -FAR, 0.0)
    factor = math.log2(math.e) / math.sqrt(HEAD_DIM)

    def head_step(h, carry):
        entry = HEAD_AT + h * FIELDS
        units = meta_ref[entry + UNITS]
        first = meta_ref[entry + FIRST]
        off = meta_ref[entry + OFFSET]
        some = before_ref[jnp.clip(meta_ref[entry + REACH], begin, stop) - begin]
        pair = h >> 1
        side = h & 1

        def attend(u, steps):
            size = u * per
            tile = min(size * min(8, pl.next_power_of_2(stop - begin)), rows)
            group = tile // size
            parts = some * steps
            tiles = (parts + (group - 1)) >> (group.bit_length() - 1)
            ours = (lane >= HALF) == (side == 1)

            for i, kv_ref in enumerate(kv_refs):
                at = before_ref[i]

                @pl.when((before_ref[i + 1] > at) & (at < some))
                def _(kv_ref=kv_ref, at=at):
                    def take(c, carry):
                        to = (at * steps + c) * size
                        keys_ref[pl.ds(pl.multiple_of(to, size), size), :] = kv_ref[
                            pl.ds(pl.multiple_of(off + c * size, per), size), :
                        ]
                        return carry

                    lax.fori_loop(0, steps, take, 0)

            def fill(i, carry):
                keys_ref[pl.ds(pl.multiple_of(i * size, size), size), :] = jnp.broadcast_to(
                    nothing, (size, LANES)
                ).astype(BF16)
                return carry

            lax.fori_loop(parts, tiles * group, fill, 0)

            def q_step(i, carry):
                here = pl.ds(pl.multiple_of(first + i * size, per), size)
                q = q_ref[h, here, :]
                acc_ref[0:size, :] = jnp.zeros((size, LANES), F32) if begin == 0 else acc_in_ref[h, here, :]

                def k_step(t, carry):
                    kv = keys_ref[pl.ds(pl.multiple_of(t * tile, tile), tile), :]
                    e = jnp.exp2(dot(q, kv, ((1,), (1,))) * factor)
                    acc_ref[0:size, :] += dot(e.astype(BF16), kv)
                    return carry

                lax.fori_loop(0, tiles, k_step, 0)
                acc = acc_ref[0:size, :]
                if begin == 0:
                    acc_out_ref[h, here, :] = acc
                total = acc[:, ONE_AT : ONE_AT + 1]
                safe = jnp.where(total > 0, total, 1.0)
                res = jnp.where(total > 0, acc / safe, 0.0).astype(BF16)
                out_ref[pair, here, :] = jnp.where(ours, res, out_ref[pair, here, :])
                return carry

            lax.fori_loop(0, steps, q_step, 0)

        for u in (1, 2, 4):
            pl.when((units == u) & (some > 0))(functools.partial(attend, u, jnp.int32(1)))
        pl.when((units >= 8) & (some > 0))(functools.partial(attend, 8, units >> 3))
        return carry

    lax.fori_loop(0, heads, head_step, 0)


def away_kernel(slides, len_ref, tok_sums_ref, out_ref, wide_ref, terms_ref, sums_ref):
    pairs, rows, _ = out_ref.shape
    width = wide_ref.shape[1]
    cols = terms_ref.shape[1]
    half = lax.axis_index("head")
    my_start = lax.axis_index(("ctx", "sub")) * rows
    tok = lax.broadcasted_iota(I32, (1, rows), 1)
    per = rows // RES
    tok = my_start + RES * (tok & (per - 1)) + rev_traced(tok // per)
    member = members(len_ref, tok, slides)
    if cols == width:
        columns = slice(None)
        own = jnp.broadcast_to(half == 0, (1, width))
    else:
        columns = pl.ds(pl.multiple_of((1 - half) * cols, LANES), cols)
        lane = lax.broadcasted_iota(I32, (1, width), 1)
        own = (lane >= half * cols) & (lane < half * cols + cols)
    sums = jnp.where(own, tok_sums_ref[:, :width], 0.0)
    for pair in range(pairs):
        pooled = dot(member, out_ref[pair])
        top = pooled.astype(BF16)
        rest = (pooled - top.astype(F32)).astype(BF16)
        both = dot(jnp.concatenate([top, rest], axis=0), wide_ref[pair * LANES : (pair + 1) * LANES, :])
        sums = sums + both[:slides] + both[slides:]
    sums_ref[:, :width] = sums
    sums_ref[:, width:] = tok_sums_ref[:, width:]
    out = jnp.concatenate([out_ref[pair] for pair in range(pairs)], axis=1)
    terms_ref[...] = dot(out, wide_ref[:, columns]).astype(BF16)


def unpermute(values, p_ref):
    rows = values.shape[0]
    per = rows // RES
    for c in range(values.shape[1] // LANES):
        for r in range(RES):
            at = rev(r) * per
            p_ref[c, pl.ds(r, per, stride=RES), :] = values[at : at + per, c * LANES : (c + 1) * LANES]


def own_kernel(x_ref, out_ref, wide_ref, y_ref, p_ref):
    pairs = out_ref.shape[0]
    cols = y_ref.shape[1]
    mine = pl.multiple_of(lax.axis_index("head") * cols, LANES)
    out = jnp.concatenate([out_ref[pair] for pair in range(pairs)], axis=1)
    unpermute(dot(out, wide_ref[:, pl.ds(mine, cols)]), p_ref)
    for c in range(cols // LANES):
        x = x_ref[:, pl.ds(pl.multiple_of(mine + c * LANES, LANES), LANES)]
        y_ref[:, c * LANES : (c + 1) * LANES] = x.astype(F32) + p_ref[c]


def mix_kernel(y_ref, got_ref, mixed_ref, p_ref):
    unpermute(got_ref[...].astype(F32), p_ref)
    for c in range(y_ref.shape[1] // LANES):
        lanes = slice(c * LANES, (c + 1) * LANES)
        mixed_ref[:, lanes] = (y_ref[:, lanes] + p_ref[c]).astype(BF16)


def loss_kernel(swapped, len_ref, pairs_ref, scale_ref, sums_ref, other_ref, *rest):
    reps, (sim_ref, loss_ref) = rest[:-2], rest[-2:]
    slides = sums_ref.shape[0]
    bank, cols = reps[0].shape
    width = sums_ref.shape[1] - bank
    row = lax.broadcasted_iota(I32, (slides, 1), 0)
    count = jnp.zeros((slides, 1), I32)
    pick = jnp.zeros((slides, 1), I32)
    for s in range(slides):
        count = jnp.where(row == s, len_ref[s], count)
        pick = jnp.where(row == s, pairs_ref[s], pick)
    dots = jnp.zeros((slides, bank), F32)
    ss = jnp.zeros((slides, 1), F32)
    for i, rep in enumerate(reps):
        at = pl.ds(0, cols)
        if swapped:
            half = lax.axis_index("head")
            at = pl.ds(pl.multiple_of((half if i == 0 else 1 - half) * cols, LANES), cols)
        sums = sums_ref[:, at]
        if swapped:
            sums = sums + other_ref[:, at]
        pooled = sums / count.astype(F32)
        ss = ss + jnp.sum(pooled * pooled, axis=1, keepdims=True)
        pieces = []
        left = pooled
        for _ in range(3):
            pieces.append(left.astype(BF16))
            left = left - pieces[-1].astype(F32)
        both = dot(jnp.concatenate(pieces, axis=0), rep[...], ((1,), (1,)))
        dots = dots + both[:slides] + both[slides : 2 * slides] + both[2 * slides :]
    rr = sums_ref[:, width:]
    if swapped:
        rr = rr + other_ref[:, width:]
    scale = jnp.exp(jnp.full((1, 1), scale_ref[0], F32))
    sim = scale * dots / jnp.sqrt((ss + 1e-06) * (rr + 1e-06))
    sim_ref[...] = sim
    total = jnp.sum(jnp.exp(sim - scale), axis=1, keepdims=True)
    lane = lax.broadcasted_iota(I32, (slides, bank), 1)
    picked = jnp.sum(jnp.where(lane == pick, sim, 0.0), axis=1, keepdims=True)
    loss = scale + jnp.log(total) - picked
    here = lax.broadcasted_iota(I32, (slides, slides), 0) == lax.broadcasted_iota(I32, (slides, slides), 1)
    loss_ref[...] = jnp.sum(jnp.where(here, loss, 0.0), axis=0)


SMEM = pl.BlockSpec(memory_space=pltpu.SMEM)
VMEM = pl.BlockSpec(memory_space=pltpu.VMEM)
ANY = pl.BlockSpec(memory_space=pl.ANY)
HBM = pl.BlockSpec(memory_space=pltpu.HBM)


def call(kernel, out_shape, in_specs, out_specs, scratch=(), grid=(), vmem=16, flops=1000000, moved=1000000):
    return pl.pallas_call(
        kernel,
        grid=grid,
        out_shape=out_shape,
        in_specs=in_specs,
        out_specs=out_specs,
        scratch_shapes=list(scratch),
        compiler_params=pltpu.CompilerParams(vmem_limit_bytes=vmem * MIB),
        cost_estimate=pl.CostEstimate(flops=flops, bytes_accessed=moved, transcendentals=0),
    )


def ladder_of(full):
    steps = ((96, 38, 18), (96, 42, 21), (96, 50, 25), (96, 58, 29), (96, 68, 34), (96, 82, 41), (96, 82, 58))
    fitting = tuple(step for step in steps if step[0] < full)
    return fitting + ((full, full, full),)


def plane(w3, which):
    return pl.BlockSpec((1,) + w3.shape[1:], lambda i: (which, 0, 0))


def run_device(
    tokens, norm_gain, w_qkv, q_gain, k_gain, w_out, seg_len, dilation, slide_len, reports, pairs, log_scale
):
    rows, width = tokens.shape
    feat = w_qkv.shape[2]
    heads = feat // HEAD_DIM
    slides = slide_len.shape[0]
    per = rows // RES
    nz, ns, nx = lax.axis_size("ctx"), lax.axis_size("sub"), lax.axis_size("head")
    blocks = nz * ns
    classes = blocks.bit_length() - 1
    full = heads * RES
    ladder = ladder_of(full)
    cols = width // nx
    swap = [(0, 1), (1, 0)]

    w3 = jnp.transpose(w_qkv, (1, 0, 2))
    pack, normed, meta = call(
        functools.partial(keys_kernel, ladder, heads, nx, classes, slides),
        (
            jax.ShapeDtypeStruct((full * per, LANES), BF16),
            jax.ShapeDtypeStruct((rows, width), BF16),
            jax.ShapeDtypeStruct((HEAD_AT + heads * FIELDS,), I32),
        ),
        [HBM] * 7,
        (VMEM, VMEM, SMEM),
        [
            pltpu.VMEM((width // LANES, rows, LANES), F32),
            pltpu.VMEM((heads, rows, LANES), BF16),
            pltpu.VMEM((rows, width), BF16),
            pltpu.VMEM((2, width, feat) if feat % LANES else (width, 2 * feat), BF16),
            pltpu.SMEM(seg_len.shape, I32),
            pltpu.SMEM(dilation.shape, I32),
            pltpu.SMEM(slide_len.shape, I32),
            pltpu.VMEM((width,), F32),
            pltpu.VMEM((feat,), F32),
            pltpu.SemaphoreType.DMA((8,)),
        ],
    )(*(pltpu.with_memory_space_constraint(a, pltpu.HBM) for a in (seg_len, dilation, slide_len, tokens, norm_gain, w3, k_gain)))

    bank = reports.shape[0]

    def branch(caps):
        near, mid, far = (min(c, full) * per for c in caps)

        def run(operands):
            pack, normed, tokens, w3, q_gain, w_out, reports, meta, slide_len = operands
            got = {0: pack}
            for m in range(1, nz):
                ends = [(i, i ^ m) for i in range(nz) if abs(i - (i ^ m)) <= nz // 2]
                got[2 * m] = lax.ppermute(pack[: mid if m == 1 else far], "ctx", ends)
            got[1] = lax.ppermute(pack[:near], "sub", swap)
            if nx == 2:
                rep_got = lax.ppermute(reports, "head", swap)
            else:
                rep_got = lax.all_gather(reports, "head", axis=1, tiled=True)
            q, tok_sums, wide = call(
                functools.partial(queries_kernel, heads, slides, blocks),
                (
                    jax.ShapeDtypeStruct((heads, rows, LANES), BF16),
                    jax.ShapeDtypeStruct((slides, width + bank), F32),
                    jax.ShapeDtypeStruct((heads // 2 * LANES, width), BF16),
                ),
                [SMEM, VMEM, VMEM, plane(w3, 0), VMEM, VMEM, VMEM],
                (VMEM, VMEM, VMEM),
                grid=(1,),
                flops=10**9,
                moved=4 * 10**6,
            )(slide_len, tokens, normed, w3, q_gain, w_out, reports)

            def scratch(count):
                return [
                    pltpu.VMEM((pl.next_power_of_2(count) * rows, LANES), BF16),
                    pltpu.VMEM((8 * per, LANES), F32),
                    pltpu.SMEM((count + 1,), I32),
                ]

            kept = jax.ShapeDtypeStruct((heads // 2, rows, LANES), BF16)
            out, acc = call(
                functools.partial(attend_kernel, heads, blocks, 0, slides),
                (kept, jax.ShapeDtypeStruct((heads, rows, LANES), F32)),
                [SMEM, SMEM, VMEM] + [VMEM] * 2,
                (VMEM, VMEM),
                scratch(2),
                flops=10**9,
                moved=8 * 10**6,
            )(meta, slide_len, q, got[0], got[1])
            for m in range(1, nz):
                got[2 * m + 1] = lax.ppermute(got[2 * m], "sub", swap)
            out = call(
                functools.partial(attend_kernel, heads, blocks, 2, slides),
                kept,
                [SMEM, SMEM, VMEM, VMEM, VMEM] + [VMEM] * (blocks - 2),
                VMEM,
                scratch(blocks - 2),
                vmem=10 + blocks * full * per * LANES * 2 // MIB + blocks * rows * LANES * 4 // MIB,
            )(meta, slide_len, q, out, acc, *(got[m] for m in range(2, blocks)))
            return out, tok_sums, wide, rep_got

        return run

    out, tok_sums, wide, rep_got = lax.switch(
        meta[0],
        [branch(caps) for caps in ladder],
        (pack, normed, tokens, w3, q_gain, w_out, reports, meta, slide_len),
    )
    terms, sums = call(
        functools.partial(away_kernel, slides),
        (
            jax.ShapeDtypeStruct((rows, cols if nx == 2 else width), BF16),
            jax.ShapeDtypeStruct((slides, width + bank), F32),
        ),
        [SMEM, VMEM, VMEM, VMEM],
        (VMEM, VMEM),
    )(slide_len, tok_sums, out, wide)
    if nx == 2:
        sums = sums + lax.ppermute(sums, "head", swap)
        got = lax.ppermute(terms, "head", swap)
        other = lax.ppermute(sums, "sub", swap)
        step = 1
        while step < nz:
            sums = sums + other
            other = lax.ppermute(sums, "ctx", [(i, i ^ step) for i in range(nz)])
            step *= 2
        unpermuted = pltpu.VMEM((cols // LANES, rows, LANES), F32)
        y = call(
            own_kernel,
            jax.ShapeDtypeStruct((rows, cols), F32),
            [VMEM] * 3,
            VMEM,
            [unpermuted],
            flops=10**9,
            moved=4 * 10**6,
        )(tokens, out, wide)
        mixed = call(
            mix_kernel,
            jax.ShapeDtypeStruct((rows, cols), BF16),
            [VMEM] * 2,
            VMEM,
            [unpermuted],
            flops=10**8,
            moved=2 * 10**6,
        )(y, got)
        reps = (reports, rep_got)
    else:
        sums = lax.psum(sums, ("ctx", "sub", "head"))
        other = sums
        back = jnp.array([rev(r) for r in range(RES)])
        terms = jnp.transpose(terms.reshape(RES, per, width)[back], (1, 0, 2)).reshape(rows, width)
        proj = lax.psum_scatter(terms, "head", scatter_dimension=1, tiled=True)
        x_cols = lax.dynamic_slice_in_dim(tokens, lax.axis_index("head") * cols, cols, 1)
        mixed = (x_cols.astype(F32) + proj.astype(F32)).astype(BF16)
        reps = (rep_got,)
    similarity, loss = call(
        functools.partial(loss_kernel, nx == 2),
        (jax.ShapeDtypeStruct((slides, bank), F32), jax.ShapeDtypeStruct((slides,), F32)),
        [SMEM, SMEM, SMEM, VMEM, VMEM] + [VMEM] * len(reps),
        (VMEM, VMEM),
    )(slide_len, pairs, log_scale, sums, other, *reps)
    return (mixed, similarity, loss)


def solution(mesh):
    in_specs = (
        P(("groups", "ctx", "sub"), None),
        P(),
        P(None, None, "head"),
        P("head"),
        P("head"),
        P("head", None),
        P(),
        P(),
        P("groups"),
        P(None, "head"),
        P("groups"),
        P(),
    )
    out_specs = (P(("groups", "ctx", "sub"), "head"), P("groups", None), P("groups"))
    return jax.shard_map(run_device, mesh=mesh, in_specs=in_specs, out_specs=out_specs, check_vma=False)
```
